32 devices in a mesh: parts: 2 (over x), rows: 16 (over z, y, core).
Axes of the slice: x: 2, y: 2, z: 4, core: 2. Of those that a mesh axis runs over, the one named last changes fastest.
Arguments:
- estimate: float32 [256, 2048], P(('parts', 'rows')), parts along dimension 0, may hold values from -6 to 6
- observed: float32 [256, 2048], P('parts', 'rows'), parts along dimension 0, may hold values from -6 to 6
- cotangent: float32 [256, 2048], P(('parts', 'rows')), parts along dimension 0
- zone_map: int32 [2, 16], P('parts'), parts along dimension 0, may hold values from 0 to 7
- bank_pick: int32 [2, 8], replicated, may hold values from 0 to 7
- psf_bank: float32 [8, 25], replicated, may hold values from 0.01 to 1
- w_first: bfloat16 [32, 1, 3, 3], replicated, may hold values from -2 to 2
- w_mid: bfloat16 [32, 32, 3, 3], replicated, may hold values from -0.375 to 0.375
- w_last: bfloat16 [1, 32, 3, 3], replicated, may hold values from -0.375 to 0.375
Outputs:
- denoised: float32 [256, 2048], P(('parts', 'rows')), parts along dimension 0
- grad_estimate: float32 [256, 2048], P(('parts', 'rows')), parts along dimension 0
- grad_first: float32 [64, 1, 3, 3], P('parts'), parts along dimension 0
- grad_mid: float32 [64, 32, 3, 3], P('parts'), parts along dimension 0
- grad_last: float32 [2, 32, 3, 3], P('parts'), parts along dimension 0
The draws below stay inside these ranges and needn't reach their ends.
There are 2 independent parts, one for each index of `parts`. The reference program is written for one: setup_inputs(seed, part) draws one part's arguments, and reference() takes and returns one part's arrays. A program takes and returns all parts, laid end to end along the dimension named above; an argument that names none is the same for every part. Nothing has to cross between parts.
All inputs are finite; a program needn't handle non-finite values.
Results may differ from the reference program's by a relative error of at most 0.0071.
Values may be sent and summed in bfloat16 or wider, within the bound.
A program may use at most 256 MiB of HBM per device.

```python
import math
import jax
import jax.numpy as jnp
from jax import lax

BLK = 128
RAD = 12
ZONES = 8
BANK = 8
CH = 32
TAPS = 25
HEIGHT = 128
WIDTH = 2048


def draw_cotangent(key, part):
    position = jnp.arange(HEIGHT, dtype=jnp.float32) / max(HEIGHT - 1, 1)
    growth = jnp.exp(math.log(3.0) * position)
    sample = jax.random.normal(key, (HEIGHT, WIDTH), jnp.float32)
    result = sample * growth[:, None] / 1.7
    return result.astype(jnp.float32)


def place_ends(drawn, own_key, low, top_value):
    shape = drawn.shape
    index_at = [jax.random.randint(jax.random.fold_in(own_key, axis), (), 0, shape[axis]) for axis in range(len(shape))]
    drawn = drawn.at[tuple(index_at)].set(low)
    longest = shape.index(max(shape))
    index_at[longest] = (index_at[longest] + 1) % shape[longest]
    return drawn.at[tuple(index_at)].set(top_value)


def levels(rng, shape, pieces, least, top_value):
    loudness = 1.0
    for dim, shards_of in pieces:
        steps = jax.random.uniform(jax.random.fold_in(jax.random.fold_in(rng, 6), dim), (shards_of,), jnp.float32, least / len(pieces), top_value / len(pieces))
        loudness = loudness * jnp.repeat(jnp.exp(steps), shape[dim] // shards_of).reshape((-1,) + (1,) * (len(shape) - 1 - dim))
    return loudness


def bell_draw(stream_key, extent, scale, most, split=(), kind=jnp.bfloat16):
    values = scale * jax.random.normal(stream_key, extent, jnp.float32)
    if split:
        values = values * levels(stream_key, extent, split, -0.22, 0.18)
    return jnp.clip(values, -most, most).astype(kind)


def setup_inputs(seed: int = 0, part: int = 0) -> dict:
    arg_keys = jax.random.split(jax.random.key(seed), 10)
    part_keys = jax.random.split(jax.random.fold_in(arg_keys[9], part), 10)
    return {
        "estimate": bell_draw(part_keys[0], (HEIGHT, WIDTH), 1.0, 6.0, ((0, 16),), jnp.float32),
        "observed": bell_draw(part_keys[1], (HEIGHT, WIDTH), 1.0, 6.0, ((1, 16),), jnp.float32),
        "cotangent": draw_cotangent(jax.random.fold_in(jax.random.fold_in(arg_keys[9], part), 71), part),
        "zone_map": place_ends(jax.random.randint(part_keys[3], (HEIGHT // BLK, WIDTH // BLK), 0, ZONES), jax.random.fold_in(part_keys[3], 1), 0, ZONES - 1).astype(jnp.int32),
        "bank_pick": place_ends(jax.random.randint(arg_keys[4], (2, ZONES), 0, BANK), jax.random.fold_in(arg_keys[4], 1), 0, BANK - 1).astype(jnp.int32),
        "psf_bank": jnp.clip(jnp.exp(jax.random.uniform(arg_keys[5], (BANK, TAPS), jnp.float32, math.log(0.01), math.log(1.0))), 0.01, 1.0),
        "w_first": bell_draw(arg_keys[6], (CH, 1, 3, 3), 9 ** -0.5, 2.0),
        "w_mid": bell_draw(arg_keys[7], (CH, CH, 3, 3), (9 * CH) ** -0.5, 0.375),
        "w_last": bell_draw(arg_keys[8], (1, CH, 3, 3), (9 * CH) ** -0.5, 0.375),
    }


STEP_SIZE = 2.0
GRAD_FACTOR = 8.0

def silu_slope(values):
    sigmoid = jax.nn.sigmoid(values)
    return sigmoid * (1.0 + values * (1.0 - sigmoid))

def flipped(weight):
    return jnp.transpose(jnp.flip(weight, (2, 3)), (1, 0, 2, 3))

def conv_rows(padded, weight):
    result = lax.conv_general_dilated(padded[None], weight, (1, 1), ((0, 0), (1, 1)), dimension_numbers=('NCHW', 'OIHW', 'NCHW'), preferred_element_type=jnp.float32)
    return result[0]

def weight_grad(padded, errors):
    framed = jnp.pad(padded, ((0, 0), (0, 0), (1, 1)))
    result = lax.conv_general_dilated(framed[None], errors[None], (1, 1), 'VALID', dimension_numbers=('CNHW', 'IOHW', 'NCHW'), preferred_element_type=jnp.float32)
    return jnp.transpose(result, (1, 0, 2, 3))

def blur_full(values, coef_at, along, adjoint):
    length = values.shape[along]
    widths = [(0, 0), (0, 0)]
    widths[along] = (RAD, RAD)
    summed = jnp.zeros_like(values)
    padded = jnp.pad(values, widths)
    for offset in range(2 * RAD + 1):
        factor = coef_at(offset)
        if adjoint:
            spread = jnp.pad(factor * values, widths)
            summed = summed + lax.slice_in_dim(spread, 2 * RAD - offset, 2 * RAD - offset + length, axis=along)
        else:
            summed = summed + factor * lax.slice_in_dim(padded, offset, offset + length, axis=along)
    return summed

def reference(estimate, observed, cotangent, zone_map, bank_pick, psf_bank, w_first, w_mid, w_last):
    norm_bank = psf_bank / lax.optimization_barrier(jnp.sum(psf_bank, axis=1, keepdims=True))
    kernels = norm_bank[bank_pick]
    zone_full = jnp.repeat(jnp.repeat(zone_map, BLK, axis=0), BLK, axis=1)

    def row_coef(offset):
        return kernels[0, :, offset][zone_full]

    def col_coef(offset):
        return kernels[1, :, offset][zone_full]

    def gradient_of(values, target):
        blurred = blur_full(values, row_coef, 1, False)
        blurred = blur_full(blurred, col_coef, 0, False)
        if target is not None:
            blurred = blurred - target
        spread = blur_full(blurred, col_coef, 0, True)
        return blur_full(spread, row_coef, 1, True)
    data_step = estimate - STEP_SIZE * gradient_of(estimate, observed)
    block_rows = BLK
    block_count = HEIGHT // block_rows
    step_pad = jnp.pad(data_step, ((4, 4), (0, 0)))
    cot_pad = jnp.pad(cotangent, ((3, 3), (0, 0)))

    def one_block(carry, block_index):
        first_row = block_index * block_rows
        step_ext = lax.dynamic_slice_in_dim(step_pad, first_row, block_rows + 8, 0)
        cot_ext = lax.dynamic_slice_in_dim(cot_pad, first_row, block_rows + 6, 0)

        def inside(offset, count_rows):
            row_ids = first_row + offset + jnp.arange(count_rows, dtype=jnp.int32)
            return ((row_ids >= 0) & (row_ids < HEIGHT)).astype(jnp.bfloat16)[None, :, None]
        first_in = step_ext.astype(jnp.bfloat16)[None]
        pre_first = conv_rows(first_in, w_first)
        act_first = jax.nn.silu(pre_first).astype(jnp.bfloat16) * inside(-3, block_rows + 6)
        pre_mid = conv_rows(act_first, w_mid)
        act_mid = jax.nn.silu(pre_mid).astype(jnp.bfloat16) * inside(-2, block_rows + 4)
        denoised = step_ext[4:4 + block_rows] + conv_rows(act_mid[:, 1:block_rows + 3], w_last)[0]
        cot_in = cot_ext.astype(jnp.bfloat16)[None]
        back_mid = (conv_rows(cot_in, flipped(w_last)) * silu_slope(pre_mid)).astype(jnp.bfloat16) * inside(-2, block_rows + 4)
        back_first = (conv_rows(back_mid, flipped(w_mid)) * silu_slope(pre_first[:, 2:block_rows + 4])).astype(jnp.bfloat16) * inside(-1, block_rows + 2)
        grad_data = cot_ext[3:3 + block_rows] + conv_rows(back_first, flipped(w_first))[0]
        grad_last = weight_grad(act_mid[:, 1:block_rows + 3], cot_in[:, 3:3 + block_rows])
        grad_mid = weight_grad(act_first[:, 2:block_rows + 4], back_mid[:, 2:2 + block_rows])
        grad_first = weight_grad(first_in[:, 3:block_rows + 5], back_first[:, 1:1 + block_rows])
        carry = (carry[0] + grad_first, carry[1] + grad_mid, carry[2] + grad_last)
        return (carry, (denoised, grad_data))
    start_sums = (jnp.zeros(w_first.shape, jnp.float32), jnp.zeros(w_mid.shape, jnp.float32), jnp.zeros(w_last.shape, jnp.float32))
    sums, outputs = lax.scan(one_block, start_sums, jnp.arange(block_count, dtype=jnp.int32))
    denoised = outputs[0].reshape(HEIGHT, WIDTH)
    grad_data = outputs[1].reshape(HEIGHT, WIDTH)
    grad_scale = GRAD_FACTOR / math.sqrt(HEIGHT * WIDTH)
    grad_estimate = grad_data - STEP_SIZE * gradient_of(grad_data, None)
    return (denoised, grad_estimate, sums[0] * grad_scale, sums[1] * grad_scale, sums[2] * grad_scale)
```

```python
import functools
import math

import jax
import jax.numpy as jnp
from jax import lax
from jax.experimental import pallas as pl
from jax.experimental.pallas import tpu as pltpu
from jax.sharding import PartitionSpec as P

BLK = 128
RAD = 12
TAPS = 2 * RAD + 1
CH = 32
BAND = 8
STEP_SIZE = 2.0
GRAD_FACTOR = 8.0
MESH = pl.DeviceIdType.MESH
F32 = jnp.float32
BF16 = jnp.bfloat16

EDGE = 16
WIDE = BLK + 2 * EDGE
NEAR = 32
COLS_PRE, COLS_MID, COLS_BACK = 70, 68, 66


def tn_dot(a, b, **kw):
    return lax.dot_general(a, b, (((0,), (0,)), ((), ())), preferred_element_type=F32, **kw)


def nt_dot(a, b):
    return lax.dot_general(a, b, (((1,), (1,)), ((), ())), preferred_element_type=F32)


def dot(a, b, **kw):
    return jnp.dot(a, b, preferred_element_type=F32, **kw)


def iota(shape, dim):
    return lax.broadcasted_iota(jnp.int32, shape, dim)


def third(v, size):
    return (v >= size).astype(jnp.int32) + (v >= 2 * size).astype(jnp.int32)


def ones_where(cond):
    return jnp.where(cond, 1.0, 0.0).astype(BF16)


def silu_pair_of_half(h):
    t = jnp.tanh(h)
    q = 0.5 * t
    act = h + h * t
    return act, (0.5 + q) + act * (0.5 - q)


def moved(v, delta, height):
    parts = []
    for at in range(0, v.shape[1], height):
        part = v[:, at : at + height]
        lane = iota((1, height), 1)
        edge = height - 1 if delta == 1 else 0
        keep = jnp.where(lane == edge, 0.0, 1.0).astype(v.dtype)
        parts.append(pltpu.roll(part, height - 1 if delta == 1 else 1, 1) * keep)
    return jnp.concatenate(parts, axis=1)


def build_weights(wf_ref, wl_ref, w9_ref, w1, wlt, wl3, wf3, wmb, wmtb):
    wf, wl = [
        jnp.concatenate([ref[0, a].astype(F32) for a in range(3)], axis=0).astype(BF16) for ref in (wf_ref, wl_ref)]

    def taps(shape, dim):
        k = iota(shape, dim)
        ka = third(k, 3)
        return ka, k - 3 * ka

    ka, kb = taps((9, 48), 0)
    lane = iota((9, 48), 1)
    la = third(lane, 16)
    lc = lane - 16 * la
    for r in range(8):
        pick = ones_where(jnp.logical_and(ka == la, kb == lc - r)) * 0.5
        w1[r * 32 : r * 32 + 32, :] = tn_dot(wf, pick.astype(BF16)).astype(BF16)
    ka, kb = taps((9, 32), 0)
    lane = iota((9, 32), 1)
    la = third(lane, 8)
    lc = lane - 8 * la
    for r in range(6):
        pick = ones_where(jnp.logical_and(jnp.logical_and(ka == la, lane < 24), kb == r + 2 - lc))
        wlt[r * 32 : r * 32 + 32, :] = tn_dot(wl, pick).astype(BF16)
    ka, kb = taps((24, 9), 1)
    out = iota((24, 9), 0)
    oa = third(out, 8)
    orow = out - 8 * oa
    for q in range(10):
        fwd = ones_where(jnp.logical_and(ka == oa, kb == q - orow))
        wl3[:, q * 32 : q * 32 + 32] = dot(fwd, wl).astype(BF16)
        adj = ones_where(jnp.logical_and(ka == oa, kb == orow + 2 - q))
        wf3[:, q * 32 : q * 32 + 32] = dot(adj, wf).astype(BF16)
    eye = ones_where(iota((32, 32), 0) == iota((32, 32), 1))
    wmb[...] = jnp.zeros_like(wmb)
    wmtb[...] = jnp.zeros_like(wmtb)
    for a in range(3):
        line = jnp.concatenate([w9_ref[a * 3 + b] for b in range(3)], axis=1)
        line = (line.astype(F32) * 0.5).astype(BF16)
        turned = [nt_dot(eye, w9_ref[a * 3 + 2 - q]) for q in range(3)]
        turned = jnp.concatenate(turned, axis=1).astype(BF16)
        for r in range(6):
            wmb[a, r * 32 : r * 32 + 32, r * 32 : r * 32 + 96] = line
            wmtb[a, r * 32 : r * 32 + 32, r * 32 : r * 32 + 96] = turned


def kernel(
    n, scale,
    est_hbm, obs_hbm, cot_hbm, zone_hbm, pick_hbm, psf_hbm, wf_hbm, wl_hbm, w9_hbm,
    den_ref, ge_ref, gm_ref, gf_ref, gl_ref,
    est_ref, obs_ref, cot_in_ref, zone_ref, pick_ref, psf_ref, wf_ref, wl_ref, w9_ref, load_sems,
    send_e, recv_e, send_c, recv_c, send_d, back_d, send_g, back_g,
    share, share_in, chip, chips, whole,
    strip, halo, strip_g, halo_g,
    tt, t2, tg, mats, ds_ref, rp_ref, cot_ref, fw, cw, slab,
    w1, wlt, wl3, wf3, wmb, wmtb, slope1, x3, x3b, mid, bfr, d24, gm_acc, gf_acc, gl_acc,
    send_sems, recv_sems, hs, hr,
):
    me = lax.axis_index("rows")
    height = BAND * n
    blocks = height // BLK
    width = BLK * n
    lanes = 2 * height
    first, last = me == 0, me == n - 1
    started = []

    def peer(k):
        return lax.rem(me + k, n)

    loads = []
    for i, (src, dst) in enumerate((
            (est_hbm, est_ref), (cot_hbm, cot_in_ref), (zone_hbm, zone_ref), (pick_hbm, pick_ref), (psf_hbm, psf_ref),
            (obs_hbm, obs_ref), (wf_hbm, wf_ref), (wl_hbm, wl_ref), (w9_hbm, w9_ref))):
        loads.append(pltpu.make_async_copy(src, dst, load_sems.at[i]))
        loads[-1].start()

    barrier = pltpu.get_barrier_semaphore()
    for k in range(1, n):
        pl.semaphore_signal(barrier, inc=1, device_id={"rows": peer(k)}, device_id_type=MESH)

    def exchange(index, src_at, dst):
        copies = []
        for k in range(1, n):
            to = peer(k)
            copies.append(pltpu.make_async_remote_copy(
                src_ref=src_at(to), dst_ref=dst.at[me],
                send_sem=send_sems.at[index, k - 1], recv_sem=recv_sems.at[index, k - 1],
                device_id={"rows": to}, device_id_type=MESH))
        for copy in copies:
            copy.start()
        started.extend(copies)
        return copies

    def neighbours(index, src, dst):
        def copy(side):
            return pltpu.make_async_remote_copy(
                src_ref=src.at[side], dst_ref=dst.at[side],
                send_sem=hs.at[index, side], recv_sem=hr.at[index, side],
                device_id={"rows": lax.rem(me + (1, n - 1)[side], n)}, device_id_type=MESH)

        sends, takes = (me < n - 1, me > 0), (me > 0, me < n - 1)
        for side in range(2):
            @pl.when(sends[side])
            def _():
                copy(side).start()

            @pl.when(jnp.logical_not(takes[side]))
            def _():
                dst[side] = jnp.zeros(dst.shape[1:], dst.dtype)

        def received():
            for side in range(2):
                @pl.when(takes[side])
                def _():
                    copy(side).wait_recv()

        def sent():
            for side in range(2):
                @pl.when(sends[side])
                def _():
                    copy(side).wait_send()

        return received, sent

    def arrive(copies):
        for copy in copies:
            copy.wait_recv()

    for copy in loads[0:2]:
        copy.wait()
    lane = iota((BAND, BLK), 1)
    zero = jnp.zeros((BAND, BLK), F32)
    hi, lo, ct = [zero], [zero], [zero]
    for g in range(n):
        own = est_ref[:, g * BLK : g * BLK + BLK]
        hi.append(own.astype(BF16).astype(F32))
        lo.append(own - hi[-1])
        ct.append(cot_in_ref[:, g * BLK : g * BLK + BLK])
    hi, lo, ct = hi + [zero], lo + [zero], ct + [zero]
    for g in range(n):
        p, c, q = g, g + 1, g + 2
        around = jnp.where(lane < 64, hi[q], hi[p])
        around = jnp.where(jnp.logical_and(lane >= 32, lane < 96), jnp.where(
            lane < 64, pltpu.roll(lo[q], 32, 1), pltpu.roll(lo[p], BLK - 32, 1)), around)
        around = jnp.where(jnp.logical_and(lane >= 40, lane < 88), jnp.where(
            lane < 64, pltpu.roll(ct[q], 40, 1), pltpu.roll(ct[p], BLK - 40, 1)), around)
        send_e[g] = jnp.concatenate([hi[c], around, lo[c]], axis=1).astype(BF16)
        send_c[g] = ct[c].astype(BF16)
    pl.semaphore_wait(barrier, n - 1)
    copies_e = exchange(0, lambda to: send_e.at[to], recv_e)
    copies_c = exchange(1, lambda to: send_c.at[to], recv_c)
    recv_e[me] = send_e[me]
    recv_c[me] = send_c[me]
    for copy in loads[2:]:
        copy.wait()

    psf = psf_ref[...]
    norm = psf / jnp.sum(psf, axis=1, keepdims=True)
    bank = iota((8, TAPS), 0)
    left, right = jnp.maximum(me - 1, 0), jnp.minimum(me + 1, n - 1)

    def taps_of(which, blk, group):
        k = pick_ref[which, zone_ref[blk, group]]
        return jnp.sum(jnp.where(bank == k, norm, 0.0), axis=0, keepdims=True)

    def banded(parts, wide, at):
        ahead = at % 8
        lines = []
        for taps, count in parts:
            line = [taps, jnp.zeros((1, wide - TAPS - ahead), F32)]
            line = jnp.concatenate([jnp.zeros((1, ahead), F32)] * (ahead > 0) + line, axis=1)
            lines.append(jnp.broadcast_to(line, (count, wide)))
        lines = lines[0] if len(lines) == 1 else jnp.concatenate(lines, axis=0)
        return pltpu.roll(lines, (at - ahead) % wide, 1, stride=1, stride_axis=0)

    for blk in range(blocks):
        parts = [
            (jnp.where(first, 0.0, taps_of(0, blk, left)), EDGE), (taps_of(0, blk, me), BLK),
            (jnp.where(last, 0.0, taps_of(0, blk, right)), EDGE)]
        tt[blk] = banded(parts, 256, -28).astype(BF16)
        turned = jnp.concatenate([banded(parts, 256, -24), jnp.zeros((256 - WIDE, 256), F32)], axis=0).T
        t2[blk] = (turned[0:144, 0:WIDE] * -STEP_SIZE).astype(BF16)
        lane = iota((WIDE, 256), 1)
        gone = jnp.logical_or(jnp.logical_and(lane < NEAR, first), jnp.logical_and(lane >= NEAR + BLK, last))
        tg[blk] = jnp.where(gone, 0.0, banded(parts, 256, 4)).astype(BF16)

    def column_operator(group):
        parts = [(taps_of(1, blk, group), BLK) for blk in range(blocks)]
        return banded(parts, height + BLK, -RAD)[:, 0:height]

    own = column_operator(me)
    target = tn_dot(obs_ref[...].astype(BF16), own.astype(BF16))
    strip[0] = target[BLK - EDGE : BLK, :].astype(BF16)
    strip[1] = target[0:EDGE, :].astype(BF16)
    received_o, sent_o = neighbours(0, strip, halo)
    slab[0:BLK, :] = target
    for i, op in enumerate((column_operator(left), own, column_operator(right))):
        mats[i] = tn_dot(op, op, precision=lax.Precision.HIGHEST).astype(BF16)
    build_weights(wf_ref, wl_ref, w9_ref, w1, wlt, wl3, wf3, wmb, wmtb)
    row, lane = iota((144, 384), 0), iota((144, 384), 1)
    rest = jnp.where(row < 4, row + 220, jnp.where(row < 132, row + 252, row + 28))
    sel = ones_where(jnp.logical_or(jnp.bitwise_and(row - 4, 255) == lane, rest == lane))
    row, lane = iota((144, 256), 0), iota((144, 256), 1)
    sel_c = ones_where(jnp.where(row < 4, row + 212, jnp.where(row < 132, row - 4, row + 36)) == lane)
    eye = ones_where(iota((BLK, BLK), 0) == iota((BLK, BLK), 1))

    def twice(v):
        return jnp.concatenate(
            [dot(v[0:EDGE], mats[0]), dot(v[EDGE : EDGE + BLK], mats[1]), dot(v[EDGE + BLK : WIDE], mats[2])], axis=0)

    def gather(ref, blk):
        per = BLK // BAND
        return jnp.concatenate([ref[blk * per + i].astype(F32) for i in range(per)], axis=0).astype(BF16)

    def joined(parts):
        return parts[0] if len(parts) == 1 else jnp.concatenate(parts, axis=1)

    def halves(v):
        low = jnp.concatenate([v[0:72], v[64:136]], axis=1)
        return jnp.concatenate([low, jnp.zeros((8, lanes), F32)], axis=0)

    arrive(copies_e)
    est = [gather(recv_e, blk) for blk in range(blocks)]
    blurred = joined([nt_dot(tt[blk], est[blk][:, 0:256]) for blk in range(blocks)]).astype(BF16)
    received_o()
    target = jnp.concatenate([halo[0].astype(F32), slab[0:BLK, :], halo[1].astype(F32)], axis=0)
    spread = (twice(blurred) - target).astype(BF16)
    row = iota((144, height), 0)
    outside = jnp.logical_or(jnp.logical_and(row < 4, first), jnp.logical_and(row >= 4 + BLK, last))
    change = joined([dot(t2[blk], spread[:, blk * BLK : blk * BLK + BLK]) for blk in range(blocks)])
    rp_ref[...] = change
    ds = joined([nt_dot(sel, est[blk]) for blk in range(blocks)]) + change
    ds = halves(jnp.where(outside, 0.0, ds))
    for a in range(3):
        line = ds if a == 1 else moved(ds, a - 1, height)
        for w in range(9):
            fw[w, a * 16 : a * 16 + 16, :] = line[8 * w : 8 * w + 16].astype(BF16)

    arrive(copies_c)
    cot = joined([
        nt_dot(sel_c, jnp.concatenate([gather(recv_c, blk), est[blk][:, BLK : 2 * BLK]], axis=1))
        for blk in range(blocks)])
    cot_ref[...] = cot
    cot = halves(cot)
    lines = [moved(cot, 1, height), cot, moved(cot, -1, height)]
    pad = jnp.zeros((8, lanes), F32)
    for w in range(12):
        at = 6 * w + 1
        cw[w] = jnp.concatenate([line[at : at + 8] for line in lines] + [pad], axis=0).astype(BF16)

    half = iota((1, lanes), 1) >= height

    def masked(v, start, begin, end):
        col = iota(v.shape, 0) // CH + start
        gone = jnp.logical_or(
            jnp.logical_and(jnp.logical_and(col < begin, first), jnp.logical_not(half)),
            jnp.logical_and(jnp.logical_and(col >= end, last), half))
        return jnp.where(gone, 0.0, v)

    def rows(at, count):
        return pl.ds(at if isinstance(at, int) else pl.multiple_of(at, 64), count)

    def conv_first(w, cols, edge):
        size = cols * CH
        act, slope = silu_pair_of_half(dot(w1[0:size, :], fw[w]))
        if edge:
            act = masked(act, 8 * w, 3, COLS_PRE - 3)
        act = act.astype(BF16)
        at = rows(w * 256, size)
        slope1[at, :] = slope.astype(BF16)
        x3[0, at, :] = moved(act, -1, height)
        x3[1, at, :] = act
        x3[2, at, :] = moved(act, 1, height)

    def run(body, count, tail, per):
        body(0, tail[0], True)
        inner = (count - 2) // per * per

        @pl.loop(0, inner // per)
        def _(i):
            for k in range(per):
                body(1 + i * per + k, tail[0], False)

        for w in range(1 + inner, count - 1):
            body(w, tail[0], False)
        body(count - 1, tail[1], True)

    run(conv_first, 9, (8, 6), 2)

    def conv_mid(w, cols, edge):
        size, deep = cols * CH, (cols + 2) * CH
        at = rows(w * 192, size)
        total = dot(wmb[0, 0:size, 0:deep], x3[0, rows(w * 192, deep), :])
        for a in (1, 2):
            total = total + dot(wmb[a, 0:size, 0:deep], x3[a, rows(w * 192, deep), :])
        act, slope = silu_pair_of_half(total)
        back = dot(wlt[0:size, :], cw[w]) * slope
        if edge:
            act = masked(act, 6 * w, 2, COLS_MID - 2)
            back = masked(back, 6 * w, 2, COLS_MID - 2)
        mid[at, :] = act.astype(BF16)
        back = back.astype(BF16)
        x3b[0, at, :] = moved(back, 1, height)
        x3b[1, at, :] = back
        x3b[2, at, :] = moved(back, -1, height)

    run(conv_mid, 12, (6, 2), 2)

    gl_acc[...] = jnp.zeros_like(gl_acc)
    for w in range(8):
        d24[w] = dot(wl3[...], mid[w * 256 + 32 : w * 256 + 352, :])
    for w in range(11):
        line = cw[w]
        if w in (0, 10):
            drop = 2 if w == 0 else 7
            r = iota((32, 1), 0)
            skip = jnp.logical_or(r == drop, jnp.logical_or(r == drop + 8, r == drop + 16))
            line = line * jnp.where(skip, 0.0, 1.0).astype(BF16)
        gl_acc[...] += nt_dot(line, mid[w * 192 : w * 192 + 256, :])

    def assembled(sign):
        low, at, high = [jnp.concatenate([d24[w, a * 8 : a * 8 + 8, :] for w in range(8)], axis=0) for a in range(3)]
        total = at + moved(low, -sign, height) + moved(high, sign, height)
        return jnp.concatenate([total[:, 0:height], total[:, height:lanes]], axis=0)

    change = (rp_ref[4 : 4 + BLK, :] + assembled(1)).astype(BF16)
    for blk in range(blocks):
        turned = tn_dot(change[:, blk * BLK : blk * BLK + BLK], eye)
        for i in range(BLK // BAND):
            send_d[blk * (BLK // BAND) + i] = turned[i * 8 : i * 8 + 8, :].astype(BF16)
    copies_d = exchange(2, lambda to: send_d.at[to], back_d)
    back_d[me] = send_d[me]

    def conv_back(w, cols, edge):
        size, deep = cols * CH, (cols + 2) * CH
        total = dot(wmtb[0, 0:size, 0:deep], x3b[0, rows(w * 192, deep), :])
        for a in (1, 2):
            total = total + dot(wmtb[a, 0:size, 0:deep], x3b[a, rows(w * 192, deep), :])
        total = total * slope1[rows(w * 192 + 64, size), :].astype(F32)
        if edge:
            total = masked(total, 6 * w, 1, COLS_BACK - 1)
        bfr[rows(w * 192, size), :] = total.astype(BF16)

    run(conv_back, 11, (6, 6), 3)

    for w in range(8):
        d24[w] = dot(wf3[...], bfr[w * 256 : w * 256 + 320, :])
    conv_grad = assembled(-1)
    slab[NEAR : NEAR + BLK, :] = conv_grad + cot_ref[4 : 4 + BLK, :]
    strip_g[0] = slab[BLK : BLK + NEAR, :].astype(BF16)
    strip_g[1] = slab[NEAR : 2 * NEAR, :].astype(BF16)
    received_g, sent_g = neighbours(1, strip_g, halo_g)

    gm_acc[...] = jnp.zeros_like(gm_acc)
    gf_acc[...] = jnp.where(iota((48, 256), 1) >= CH, nt_dot(fw[0], bfr[0:256, :]), 0.0)
    for w in range(1, 8):
        gf_acc[...] += nt_dot(fw[w], bfr[w * 256 : w * 256 + 256, :])
    gf_acc[:, 0:CH] += nt_dot(fw[8], bfr[2048 : 2048 + CH, :])

    @pl.loop(0, 10)
    def _(w):
        act = x3[1, rows(w * 192 + 64, 256), :]
        for a in range(3):
            gm_acc[a] += nt_dot(x3b[a, rows(w * 192 + 64, 192), :], act)

    act = x3[1, 62 * CH : 68 * CH, :]
    for a in range(3):
        gm_acc[a, 0:128, 0:192] += nt_dot(x3b[a, 62 * CH : 66 * CH, :], act)

    share[...] = jnp.zeros_like(share)
    for a in range(3):
        for b in range(3):
            total = jnp.zeros((CH, CH), F32)
            total_first = jnp.zeros((1, CH), F32)
            total_last = jnp.zeros((1, CH), F32)
            for r in range(6):
                total = total + gm_acc[a, r * 32 : r * 32 + 32, (r + b) * 32 : (r + b) * 32 + 32]
                c = a * 8 + r + 2
                total_last = total_last + gl_acc[c : c + 1, (r + b) * 32 : (r + b) * 32 + 32]
            for r in range(8):
                c = a * 16 + r + 2 + b
                total_first = total_first + gf_acc[c : c + 1, r * 32 : r * 32 + 32]
            slot = a * 3 + b
            share[slot // 4 * 32 : slot // 4 * 32 + 32, slot % 4 * 32 : slot % 4 * 32 + 32] = total * scale
            share[64 + slot : 65 + slot, 32:64] = total_first * scale
            share[64 + slot : 65 + slot, 64:96] = total_last * scale

    core = lax.rem(me, 2)
    pair = me + 1 - 2 * core

    def part(i):
        return pl.ds(pl.multiple_of(i * 48, 16), 48)

    def to_pair(index, src, dst):
        copy = pltpu.make_async_remote_copy(
            src_ref=src, dst_ref=dst, send_sem=hs.at[2, index], recv_sem=hr.at[2, index],
            device_id={"rows": pair}, device_id_type=MESH)
        copy.start()
        started.append(copy)
        return copy

    copy_s = to_pair(0, share.at[part(1 - core)], share_in)

    received_g()
    grad = jnp.concatenate([halo_g[0], slab[NEAR : NEAR + BLK, :].astype(BF16), halo_g[1]], axis=0)
    blurred = [dot(tg[blk, :, 0:192], grad[:, blk * BLK : blk * BLK + BLK]) for blk in range(blocks)]
    spread = (twice(joined(blurred).astype(BF16)) * -STEP_SIZE).astype(BF16)
    conv_grad = conv_grad.astype(BF16)
    for blk in range(blocks):
        at = slice(blk * BLK, blk * BLK + BLK)
        change = tn_dot(spread[:, at], tt[blk, :, 0:BLK]) + tn_dot(conv_grad[:, at], eye)
        for i in range(BLK // BAND):
            send_g[blk * (BLK // BAND) + i] = change[i * 8 : i * 8 + 8, :].astype(BF16)
    copies_b = exchange(3, lambda to: send_g.at[to], back_g)
    back_g[me] = send_g[me]

    copy_s.wait_recv()
    number = me // 2
    chip[...] = (share[part(core), :] + share_in[...]).astype(BF16)
    copies_t = []
    for k in range(1, n // 2):
        copies_t.append(pltpu.make_async_remote_copy(
            src_ref=chip, dst_ref=chips.at[number],
            send_sem=send_sems.at[4, k - 1], recv_sem=recv_sems.at[4, k - 1],
            device_id={"rows": lax.rem(me + 2 * k, n)}, device_id_type=MESH))
    for copy in copies_t:
        copy.start()
    started.extend(copies_t)
    chips[number] = chip[...]
    arrive(copies_d)
    for g in range(n):
        at = slice(g * BLK, g * BLK + BLK)
        den_ref[:, at] = est_ref[:, at] + back_d[g].astype(F32)
    arrive(copies_t)
    total = chips[0].astype(F32)
    for i in range(1, n // 2):
        total = total + chips[i].astype(F32)
    whole[part(core), :] = total
    copy_w = to_pair(1, whole.at[part(core)], whole.at[part(core)])
    arrive(copies_b)
    for g in range(n):
        at = slice(g * BLK, g * BLK + BLK)
        ge_ref[:, at] = cot_in_ref[:, at] + back_g[g].astype(F32)
    copy_w.wait_recv()
    for slot in range(9):
        gm_ref[slot] = whole[slot // 4 * 32 : slot // 4 * 32 + 32, slot % 4 * 32 : slot % 4 * 32 + 32]
        gf_ref[slot] = whole[64 + slot : 65 + slot, 32:64]
        gl_ref[slot] = whole[64 + slot : 65 + slot, 64:96]
    sent_o()
    sent_g()
    for copy in started:
        copy.wait_send()


def deliver(*refs):
    sems = refs[-1]
    copies = [pltpu.make_async_copy(refs[i], refs[5 + i], sems.at[i]) for i in range(5)]
    for copy in copies:
        copy.start()
    for copy in copies:
        copy.wait()


def on_device(n, estimate, observed, cotangent, zone_map, bank_pick, psf_bank, w_first, w_mid, w_last):
    width = estimate.shape[1]
    height = BAND * n
    lanes = 2 * height
    blocks = height // BLK
    scale = GRAD_FACTOR / math.sqrt(height * width)
    vmem, hbm = pl.BlockSpec(memory_space=pltpu.VMEM), pl.BlockSpec(memory_space=pltpu.HBM)
    flat = pltpu.VMEM((n, 8, BLK), BF16)
    broad = pltpu.VMEM((n, 8, 3 * BLK), BF16)
    ends = jnp.transpose(w_first, (1, 2, 3, 0)), jnp.transpose(w_last, (0, 2, 3, 1))
    middle = jnp.transpose(w_mid, (2, 3, 0, 1)).reshape(9, CH, CH)
    operands = [
        pltpu.with_memory_space_constraint(v, pltpu.HBM)
        for v in (estimate, observed, cotangent, zone_map, bank_pick, psf_bank, *ends, middle)]
    results = pl.pallas_call(
        functools.partial(kernel, n, scale),
        out_shape=(
            pltpu.VMEM((8, width), F32),
            pltpu.VMEM((8, width), F32),
            pltpu.VMEM((9, CH, CH), F32),
            pltpu.VMEM((9, 1, CH), F32),
            pltpu.VMEM((9, 1, CH), F32),
        ),
        in_specs=[hbm] * 9,
        out_specs=[vmem] * 5,
        scratch_shapes=[
            pltpu.VMEM((8, width), F32),
            pltpu.VMEM((height, BLK), F32),
            pltpu.VMEM((8, width), F32),
            pltpu.SMEM(zone_map.shape, jnp.int32),
            pltpu.SMEM(bank_pick.shape, jnp.int32),
            pltpu.VMEM(psf_bank.shape, F32),
            pltpu.VMEM((1, 3, 3, CH), BF16),
            pltpu.VMEM((1, 3, 3, CH), BF16),
            pltpu.VMEM((9, CH, CH), BF16),
            pltpu.SemaphoreType.DMA((9,)),
            broad, broad, flat, flat, flat, flat, flat, flat,
            pltpu.VMEM((96, BLK), F32),
            pltpu.VMEM((48, BLK), F32),
            pltpu.VMEM((48, BLK), BF16),
            pltpu.VMEM((n // 2, 48, BLK), BF16),
            pltpu.VMEM((96, BLK), F32),
            pltpu.VMEM((2, EDGE, height), BF16),
            pltpu.VMEM((2, EDGE, height), BF16),
            pltpu.VMEM((2, NEAR, height), BF16),
            pltpu.VMEM((2, NEAR, height), BF16),
            pltpu.VMEM((blocks, WIDE, 256), BF16),
            pltpu.VMEM((blocks, 144, WIDE), BF16),
            pltpu.VMEM((blocks, WIDE, 256), BF16),
            pltpu.VMEM((3, height, height), BF16),
            pltpu.VMEM((144, height), F32),
            pltpu.VMEM((144, height), F32),
            pltpu.VMEM((144, height), F32),
            pltpu.VMEM((9, 48, lanes), BF16),
            pltpu.VMEM((12, 32, lanes), BF16),
            pltpu.VMEM((NEAR + BLK, height), F32),
            pltpu.VMEM((256, 48), BF16),
            pltpu.VMEM((192, 32), BF16),
            pltpu.VMEM((24, 320), BF16),
            pltpu.VMEM((24, 320), BF16),
            pltpu.VMEM((3, 192, 256), BF16),
            pltpu.VMEM((3, 192, 256), BF16),
            pltpu.VMEM((COLS_PRE * CH, lanes), BF16),
            pltpu.VMEM((3, COLS_PRE * CH, lanes), BF16),
            pltpu.VMEM((3, COLS_MID * CH, lanes), BF16),
            pltpu.VMEM((COLS_MID * CH, lanes), BF16),
            pltpu.VMEM((COLS_BACK * CH, lanes), BF16),
            pltpu.VMEM((8, 24, lanes), F32),
            pltpu.VMEM((3, 192, 256), F32),
            pltpu.VMEM((48, 256), F32),
            pltpu.VMEM((32, 256), F32),
            pltpu.SemaphoreType.DMA((5, n - 1)),
            pltpu.SemaphoreType.DMA((5, n - 1)),
            pltpu.SemaphoreType.DMA((3, 2)),
            pltpu.SemaphoreType.DMA((3, 2)),
        ],
        compiler_params=pltpu.CompilerParams(
            collective_id=0, has_side_effects=True, vmem_limit_bytes=40 << 20 if height <= 256 else 62 << 20),
    )(*operands)
    denoised, grad_estimate, grad_mid, grad_first, grad_last = pl.pallas_call(
        deliver,
        out_shape=tuple(pltpu.HBM(v.shape, v.dtype) for v in results),
        in_specs=[vmem] * 5,
        out_specs=[hbm] * 5,
        scratch_shapes=[pltpu.SemaphoreType.DMA((5,))],
    )(*[pltpu.with_memory_space_constraint(v, pltpu.VMEM) for v in results])
    grad_mid = jnp.transpose(grad_mid.reshape(3, 3, CH, CH), (2, 3, 0, 1))
    grad_first = jnp.transpose(grad_first.reshape(3, 3, 1, CH), (3, 2, 0, 1))
    grad_last = jnp.transpose(grad_last.reshape(3, 3, 1, CH), (2, 3, 0, 1))
    return denoised, grad_estimate, grad_first, grad_mid, grad_last


def solution(mesh):
    placed = (
        P(("parts", "rows"), None),
        P("parts", "rows"),
        P(("parts", "rows"), None),
        P("parts", None),
        P(), P(), P(), P(), P(),
    )
    return jax.shard_map(
        functools.partial(on_device, mesh.shape["rows"]),
        mesh=mesh,
        in_specs=placed,
        out_specs=(
            P(("parts", "rows"), None),
            P(("parts", "rows"), None),
            P("parts", None, None, None),
            P("parts", None, None, None),
            P("parts", None, None, None),
        ),
        check_vma=False,
    )
```

```python
import functools
import math

import jax
import jax.numpy as jnp
from jax import lax
from jax.experimental import pallas as pl
from jax.experimental.pallas import tpu as pltpu
from jax.sharding import PartitionSpec as P

BLK = 128
RAD = 12
TAPS = 2 * RAD + 1
CH = 32
BAND = 8
STEP_SIZE = 2.0
GRAD_FACTOR = 8.0
MESH = pl.DeviceIdType.MESH
F32 = jnp.float32
BF16 = jnp.bfloat16

EDGE = 16
WIDE = BLK + 2 * EDGE
NEAR = 32
COLS_PRE, COLS_MID, COLS_BACK = 70, 68, 66


def tn_dot(a, b, **kw):
    return lax.dot_general(a, b, (((0,), (0,)), ((), ())), preferred_element_type=F32, **kw)


def nt_dot(a, b):
    return lax.dot_general(a, b, (((1,), (1,)), ((), ())), preferred_element_type=F32)


def dot(a, b, **kw):
    return jnp.dot(a, b, preferred_element_type=F32, **kw)


def iota(shape, dim):
    return lax.broadcasted_iota(jnp.int32, shape, dim)


def third(v, size):
    return (v >= size).astype(jnp.int32) + (v >= 2 * size).astype(jnp.int32)


def ones_where(cond):
    return jnp.where(cond, 1.0, 0.0).astype(BF16)


def silu_pair_of_half(h):
    t = jnp.tanh(h)
    q = 0.5 * t
    act = h + h * t
    return act, (0.5 + q) + act * (0.5 - q)


def moved(v, delta, height):
    parts = []
    for at in range(0, v.shape[1], height):
        part = v[:, at : at + height]
        lane = iota((1, height), 1)
        edge = height - 1 if delta == 1 else 0
        keep = jnp.where(lane == edge, 0.0, 1.0).astype(v.dtype)
        parts.append(pltpu.roll(part, height - 1 if delta == 1 else 1, 1) * keep)
    return jnp.concatenate(parts, axis=1)


def build_weights(wf_ref, wl_ref, w9_ref, w1, wlt, wl3, wf3, wmb, wmtb):
    wf, wl = [
        jnp.concatenate([ref[0, a].astype(F32) for a in range(3)], axis=0).astype(BF16) for ref in (wf_ref, wl_ref)]

    def taps(shape, dim):
        k = iota(shape, dim)
        ka = third(k, 3)
        return ka, k - 3 * ka

    ka, kb = taps((9, 48), 0)
    lane = iota((9, 48), 1)
    la = third(lane, 16)
    lc = lane - 16 * la
    for r in range(8):
        pick = ones_where(jnp.logical_and(ka == la, kb == lc - r)) * 0.5
        w1[r * 32 : r * 32 + 32, :] = tn_dot(wf, pick.astype(BF16)).astype(BF16)
    ka, kb = taps((9, 32), 0)
    lane = iota((9, 32), 1)
    la = third(lane, 8)
    lc = lane - 8 * la
    for r in range(6):
        pick = ones_where(jnp.logical_and(jnp.logical_and(ka == la, lane < 24), kb == r + 2 - lc))
        wlt[r * 32 : r * 32 + 32, :] = tn_dot(wl, pick).astype(BF16)
    ka, kb = taps((24, 9), 1)
    out = iota((24, 9), 0)
    oa = third(out, 8)
    orow = out - 8 * oa
    for q in range(10):
        fwd = ones_where(jnp.logical_and(ka == oa, kb == q - orow))
        wl3[:, q * 32 : q * 32 + 32] = dot(fwd, wl).astype(BF16)
        adj = ones_where(jnp.logical_and(ka == oa, kb == orow + 2 - q))
        wf3[:, q * 32 : q * 32 + 32] = dot(adj, wf).astype(BF16)
    eye = ones_where(iota((32, 32), 0) == iota((32, 32), 1))
    wmb[...] = jnp.zeros_like(wmb)
    wmtb[...] = jnp.zeros_like(wmtb)
    for a in range(3):
        line = jnp.concatenate([w9_ref[a * 3 + b] for b in range(3)], axis=1)
        line = (line.astype(F32) * 0.5).astype(BF16)
        turned = [nt_dot(eye, w9_ref[a * 3 + 2 - q]) for q in range(3)]
        turned = jnp.concatenate(turned, axis=1).astype(BF16)
        for r in range(6):
            wmb[a, r * 32 : r * 32 + 32, r * 32 : r * 32 + 96] = line
            wmtb[a, r * 32 : r * 32 + 32, r * 32 : r * 32 + 96] = turned


def kernel(
    n, scale,
    est_hbm, obs_hbm, cot_hbm, zone_hbm, pick_hbm, psf_hbm, wf_hbm, wl_hbm, w9_hbm,
    den_ref, ge_ref, gm_ref, gf_ref, gl_ref,
    est_ref, obs_ref, cot_in_ref, zone_ref, pick_ref, psf_ref, wf_ref, wl_ref, w9_ref, load_sems,
    send_e, recv_e, send_g, back_g,
    share, share_in, chip, chips, whole,
    strip, halo, strip_g, halo_g,
    tt, t2, tg, mats, ds_ref, rp_ref, cot_ref, fw, cw, slab,
    w1, wlt, wl3, wf3, wmb, wmtb, slope1, x3, x3b, mid, bfr, d24, gm_acc, gf_acc,
    send_sems, recv_sems, hs, hr,
):
    me = lax.axis_index("rows")
    height = BAND * n
    blocks = height // BLK
    width = BLK * n
    lanes = 2 * height
    first, last = me == 0, me == n - 1
    started = []

    def peer(k):
        return lax.rem(me + k, n)

    loads = []
    for i, (src, dst) in enumerate((
            (est_hbm, est_ref), (cot_hbm, cot_in_ref), (zone_hbm, zone_ref), (pick_hbm, pick_ref), (psf_hbm, psf_ref),
            (obs_hbm, obs_ref), (wf_hbm, wf_ref), (wl_hbm, wl_ref), (w9_hbm, w9_ref))):
        loads.append(pltpu.make_async_copy(src, dst, load_sems.at[i]))
        loads[-1].start()

    barrier = pltpu.get_barrier_semaphore()
    for k in range(1, n):
        pl.semaphore_signal(barrier, inc=1, device_id={"rows": peer(k)}, device_id_type=MESH)

    def exchange(index, src_at, dst):
        copies = []
        for k in range(1, n):
            to = peer(k)
            copies.append(pltpu.make_async_remote_copy(
                src_ref=src_at(to), dst_ref=dst.at[me],
                send_sem=send_sems.at[index, k - 1], recv_sem=recv_sems.at[index, k - 1],
                device_id={"rows": to}, device_id_type=MESH))
        for copy in copies:
            copy.start()
        started.extend(copies)
        return copies

    def neighbours(index, src, dst):
        def copy(side):
            return pltpu.make_async_remote_copy(
                src_ref=src.at[side], dst_ref=dst.at[side],
                send_sem=hs.at[index, side], recv_sem=hr.at[index, side],
                device_id={"rows": lax.rem(me + (1, n - 1)[side], n)}, device_id_type=MESH)

        sends, takes = (me < n - 1, me > 0), (me > 0, me < n - 1)
        for side in range(2):
            @pl.when(sends[side])
            def _():
                copy(side).start()

            @pl.when(jnp.logical_not(takes[side]))
            def _():
                dst[side] = jnp.zeros(dst.shape[1:], dst.dtype)

        def received():
            for side in range(2):
                @pl.when(takes[side])
                def _():
                    copy(side).wait_recv()

        def sent():
            for side in range(2):
                @pl.when(sends[side])
                def _():
                    copy(side).wait_send()

        return received, sent

    def arrive(copies):
        for copy in copies:
            copy.wait_recv()

    for copy in loads[0:2]:
        copy.wait()
    lane = iota((BAND, BLK), 1)
    zero = jnp.zeros((BAND, BLK), F32)
    hi, lo, ct = [zero], [zero], [zero]
    for g in range(n):
        own = est_ref[:, g * BLK : g * BLK + BLK]
        hi.append(own.astype(BF16).astype(F32))
        lo.append(own - hi[-1])
        ct.append(cot_in_ref[:, g * BLK : g * BLK + BLK])
    hi, lo, ct = hi + [zero], lo + [zero], ct + [zero]
    for g in range(n):
        p, c, q = g, g + 1, g + 2
        around = jnp.where(lane < 64, hi[q], hi[p])
        around = jnp.where(jnp.logical_and(lane >= 32, lane < 96), jnp.where(
            lane < 64, pltpu.roll(lo[q], 32, 1), pltpu.roll(lo[p], BLK - 32, 1)), around)
        around = jnp.where(jnp.logical_and(lane >= 40, lane < 88), jnp.where(
            lane < 64, pltpu.roll(ct[q], 40, 1), pltpu.roll(ct[p], BLK - 40, 1)), around)
        send_e[g] = jnp.concatenate([hi[c], around, lo[c], ct[c]], axis=1).astype(BF16)
    pl.semaphore_wait(barrier, n - 1)
    copies_e = exchange(0, lambda to: send_e.at[to], recv_e)
    recv_e[me] = send_e[me]
    for copy in loads[2:]:
        copy.wait()

    psf = psf_ref[...]
    norm = psf / jnp.sum(psf, axis=1, keepdims=True)
    bank = iota((8, TAPS), 0)
    left, right = jnp.maximum(me - 1, 0), jnp.minimum(me + 1, n - 1)

    def taps_of(which, blk, group):
        k = pick_ref[which, zone_ref[blk, group]]
        return jnp.sum(jnp.where(bank == k, norm, 0.0), axis=0, keepdims=True)

    def banded(parts, wide, at):
        ahead = at % 8
        lines = []
        for taps, count in parts:
            line = [taps, jnp.zeros((1, wide - TAPS - ahead), F32)]
            line = jnp.concatenate([jnp.zeros((1, ahead), F32)] * (ahead > 0) + line, axis=1)
            lines.append(jnp.broadcast_to(line, (count, wide)))
        lines = lines[0] if len(lines) == 1 else jnp.concatenate(lines, axis=0)
        return pltpu.roll(lines, (at - ahead) % wide, 1, stride=1, stride_axis=0)

    for blk in range(blocks):
        parts = [
            (jnp.where(first, 0.0, taps_of(0, blk, left)), EDGE), (taps_of(0, blk, me), BLK),
            (jnp.where(last, 0.0, taps_of(0, blk, right)), EDGE)]
        tt[blk] = banded(parts, 256, -28).astype(BF16)
        turned = jnp.concatenate([banded(parts, 256, -24), jnp.zeros((256 - WIDE, 256), F32)], axis=0).T
        t2[blk] = (turned[0:144, 0:WIDE] * -STEP_SIZE).astype(BF16)
        lane = iota((WIDE, 256), 1)
        gone = jnp.logical_or(jnp.logical_and(lane < NEAR, first), jnp.logical_and(lane >= NEAR + BLK, last))
        tg[blk] = jnp.where(gone, 0.0, banded(parts, 256, 4)).astype(BF16)

    def column_operator(group):
        parts = [(taps_of(1, blk, group), BLK) for blk in range(blocks)]
        return banded(parts, height + BLK, -RAD)[:, 0:height]

    own = column_operator(me)
    target = tn_dot(obs_ref[...].astype(BF16), own.astype(BF16))
    strip[0] = target[BLK - EDGE : BLK, :].astype(BF16)
    strip[1] = target[0:EDGE, :].astype(BF16)
    received_o, sent_o = neighbours(0, strip, halo)
    slab[0:BLK, :] = target
    for i, op in enumerate((column_operator(left), own, column_operator(right))):
        mats[i] = tn_dot(op, op, precision=lax.Precision.HIGHEST).astype(BF16)
    build_weights(wf_ref, wl_ref, w9_ref, w1, wlt, wl3, wf3, wmb, wmtb)
    row, lane = iota((144, 384), 0), iota((144, 384), 1)
    rest = jnp.where(row < 4, row + 220, jnp.where(row < 132, row + 252, row + 28))
    sel = ones_where(jnp.logical_or(jnp.bitwise_and(row - 4, 255) == lane, rest == lane))
    row, lane = iota((144, 256), 0), iota((144, 256), 1)
    sel_c = ones_where(jnp.where(row < 4, row + 212, jnp.where(row < 132, row - 4, row + 36)) == lane)
    eye = ones_where(iota((BLK, BLK), 0) == iota((BLK, BLK), 1))

    def twice(v):
        return jnp.concatenate(
            [dot(v[0:EDGE], mats[0]), dot(v[EDGE : EDGE + BLK], mats[1]), dot(v[EDGE + BLK : WIDE], mats[2])], axis=0)

    def gather(blk):
        per = BLK // BAND
        return jnp.concatenate([recv_e[blk * per + i].astype(F32) for i in range(per)], axis=0).astype(BF16)

    def joined(parts):
        return parts[0] if len(parts) == 1 else jnp.concatenate(parts, axis=1)

    def halves(v):
        low = jnp.concatenate([v[0:72], v[64:136]], axis=1)
        return jnp.concatenate([low, jnp.zeros((8, lanes), F32)], axis=0)

    arrive(copies_e)
    est = [gather(blk) for blk in range(blocks)]
    blurred = joined([nt_dot(tt[blk], est[blk][:, 0:256]) for blk in range(blocks)]).astype(BF16)
    received_o()
    target = jnp.concatenate([halo[0].astype(F32), slab[0:BLK, :], halo[1].astype(F32)], axis=0)
    spread = (twice(blurred) - target).astype(BF16)
    row = iota((144, height), 0)
    outside = jnp.logical_or(jnp.logical_and(row < 4, first), jnp.logical_and(row >= 4 + BLK, last))
    change = joined([dot(t2[blk], spread[:, blk * BLK : blk * BLK + BLK]) for blk in range(blocks)])
    rp_ref[...] = change
    ds = joined([nt_dot(sel, est[blk][:, 0:384]) for blk in range(blocks)]) + change
    ds = halves(jnp.where(outside, 0.0, ds))
    for a in range(3):
        line = ds if a == 1 else moved(ds, a - 1, height)
        for w in range(9):
            fw[w, a * 16 : a * 16 + 16, :] = line[8 * w : 8 * w + 16].astype(BF16)

    cot = joined([
        nt_dot(sel_c, jnp.concatenate([est[blk][:, 3 * BLK :], est[blk][:, BLK : 2 * BLK]], axis=1))
        for blk in range(blocks)])
    cot_ref[...] = cot
    cot = halves(cot)
    lines = [moved(cot, 1, height), cot, moved(cot, -1, height)]
    pad = jnp.zeros((8, lanes), F32)
    for w in range(12):
        at = 6 * w + 1
        cw[w] = jnp.concatenate([line[at : at + 8] for line in lines] + [pad], axis=0).astype(BF16)

    half = iota((1, lanes), 1) >= height

    def masked(v, start, begin, end):
        col = iota(v.shape, 0) // CH + start
        gone = jnp.logical_or(
            jnp.logical_and(jnp.logical_and(col < begin, first), jnp.logical_not(half)),
            jnp.logical_and(jnp.logical_and(col >= end, last), half))
        return jnp.where(gone, 0.0, v)

    def rows(at, count):
        return pl.ds(at if isinstance(at, int) else pl.multiple_of(at, 64), count)

    def conv_first(w, cols, edge):
        size = cols * CH
        act, slope = silu_pair_of_half(dot(w1[0:size, :], fw[w]))
        if edge:
            act = masked(act, 8 * w, 3, COLS_PRE - 3)
        act = act.astype(BF16)
        at = rows(w * 256, size)
        slope1[at, :] = slope.astype(BF16)
        x3[0, at, :] = moved(act, -1, height)
        x3[1, at, :] = act
        x3[2, at, :] = moved(act, 1, height)

    def run(body, count, tail):
        body(0, tail[0], True)
        if blocks == 1:
            for w in range(1, count - 1):
                body(w, tail[0], False)
        else:
            @pl.loop(1, count - 1)
            def _(w):
                body(w, tail[0], False)
        body(count - 1, tail[1], True)

    run(conv_first, 9, (8, 6))

    def conv_mid(w, cols, edge):
        size, deep = cols * CH, (cols + 2) * CH
        at = rows(w * 192, size)
        total = dot(wmb[0, 0:size, 0:deep], x3[0, rows(w * 192, deep), :])
        for a in (1, 2):
            total = total + dot(wmb[a, 0:size, 0:deep], x3[a, rows(w * 192, deep), :])
        act, slope = silu_pair_of_half(total)
        back = dot(wlt[0:size, :], cw[w]) * slope
        if edge:
            act = masked(act, 6 * w, 2, COLS_MID - 2)
            back = masked(back, 6 * w, 2, COLS_MID - 2)
        mid[at, :] = act.astype(BF16)
        back = back.astype(BF16)
        x3b[0, at, :] = moved(back, 1, height)
        x3b[1, at, :] = back
        x3b[2, at, :] = moved(back, -1, height)

    run(conv_mid, 12, (6, 2))

    def conv_back(w, cols, edge):
        size, deep = cols * CH, (cols + 2) * CH
        total = dot(wmtb[0, 0:size, 0:deep], x3b[0, rows(w * 192, deep), :])
        for a in (1, 2):
            total = total + dot(wmtb[a, 0:size, 0:deep], x3b[a, rows(w * 192, deep), :])
        total = total * slope1[rows(w * 192 + 64, size), :].astype(F32)
        if edge:
            total = masked(total, 6 * w, 1, COLS_BACK - 1)
        bfr[rows(w * 192, size), :] = total.astype(BF16)

    run(conv_back, 11, (6, 6))

    def assembled(sign):
        low, at, high = [jnp.concatenate([d24[w, a * 8 : a * 8 + 8, :] for w in range(8)], axis=0) for a in range(3)]
        total = at + moved(low, -sign, height) + moved(high, sign, height)
        return jnp.concatenate([total[:, 0:height], total[:, height:lanes]], axis=0)

    for w in range(8):
        d24[w] = dot(wf3[...], bfr[w * 256 : w * 256 + 320, :])
    conv_grad = assembled(-1)
    slab[NEAR : NEAR + BLK, :] = conv_grad + cot_ref[4 : 4 + BLK, :]
    strip_g[0] = slab[BLK : BLK + NEAR, :].astype(BF16)
    strip_g[1] = slab[NEAR : 2 * NEAR, :].astype(BF16)
    received_g, sent_g = neighbours(1, strip_g, halo_g)

    def beside(parts):
        return jnp.concatenate(parts, axis=1)

    def last_dot():
        lines = []
        for w in range(11):
            line = cw[w]
            if w in (0, 10):
                drop = 2 if w == 0 else 7
                r = iota((32, 1), 0)
                skip = jnp.logical_or(r == drop, jnp.logical_or(r == drop + 8, r == drop + 16))
                line = line * jnp.where(skip, 0.0, 1.0).astype(BF16)
            lines.append(line)
        return nt_dot(beside(lines), beside([mid[w * 192 : w * 192 + 256, :] for w in range(11)]))

    def first_dot():
        gf_acc[...] = jnp.where(iota((48, 256), 1) >= CH, nt_dot(fw[0], bfr[0:256, :]), 0.0) + nt_dot(
            beside([fw[w] for w in range(1, 8)]), beside([bfr[w * 256 : w * 256 + 256, :] for w in range(1, 8)]))
        gf_acc[:, 0:CH] += nt_dot(fw[8], bfr[2048 : 2048 + CH, :])
        return gf_acc[...]

    per = 10 if blocks == 1 else 2
    for g in range(0, 10, per):
        acts = beside([x3[1, w * 192 + 64 : w * 192 + 320, :] for w in range(g, g + per)])
        backs = beside([x3b[:, w * 192 + 64 : w * 192 + 256, :].reshape(576, lanes) for w in range(g, g + per)])
        total = nt_dot(backs, acts).reshape(3, 192, 256)
        gm_acc[...] = total if g == 0 else gm_acc[...] + total
    gm_acc[:, 0:128, 0:192] += nt_dot(
        x3b[:, 62 * CH : 66 * CH, :].reshape(384, lanes), x3[1, 62 * CH : 68 * CH, :]).reshape(3, 128, 192)

    for a in range(3):
        total = gm_acc[a, 0:32, :]
        for r in range(1, 6):
            total = total + pltpu.roll(gm_acc[a, r * 32 : r * 32 + 32, :], 256 - 32 * r, 1)
        share[a * 32 : a * 32 + 32, :] = total[:, 0:BLK] * scale
    ends = []
    for acc, deep, ahead in ((first_dot(), 16, 2), (last_dot(), 8, 2)):
        acc = acc[0 : 3 * deep].reshape(3, deep, 256)
        c, col = iota((3, deep, 256), 1), iota((3, deep, 256), 2) // CH
        for b in range(3):
            hit = c == col + 2 + b if deep == 16 else jnp.logical_and(c >= 2, c - 2 + b == col)
            ends.append(jnp.sum(jnp.where(hit, acc, 0.0), axis=1))
    ends = jnp.concatenate(ends + [jnp.zeros((6, 256), F32)], axis=0)
    ends = ends[:, 0:BLK] + ends[:, BLK:]
    ends = ends + pltpu.roll(ends, 64, 1)
    ends = (ends + pltpu.roll(ends, 32, 1)) * scale
    share[0:24, 96:BLK] = ends[:, 96:BLK]

    core = lax.rem(me, 2)
    pair = me + 1 - 2 * core

    def part(i):
        return pl.ds(pl.multiple_of(i * 48, 16), 48)

    def to_pair(index, src, dst):
        copy = pltpu.make_async_remote_copy(
            src_ref=src, dst_ref=dst, send_sem=hs.at[2, index], recv_sem=hr.at[2, index],
            device_id={"rows": pair}, device_id_type=MESH)
        copy.start()
        started.append(copy)
        return copy

    copy_s = to_pair(0, share.at[part(1 - core)], share_in)

    for w in range(8):
        d24[w] = dot(wl3[...], mid[w * 256 + 32 : w * 256 + 352, :])
    conv_out = (rp_ref[4 : 4 + BLK, :] + assembled(1)).astype(BF16)
    copy_s.wait_recv()
    number = me // 2
    chip[...] = (share[part(core), :] + share_in[...]).astype(BF16)
    copies_t = []
    for k in range(1, n // 2):
        copies_t.append(pltpu.make_async_remote_copy(
            src_ref=chip, dst_ref=chips.at[number],
            send_sem=send_sems.at[1, k - 1], recv_sem=recv_sems.at[1, k - 1],
            device_id={"rows": lax.rem(me + 2 * k, n)}, device_id_type=MESH))
    for copy in copies_t:
        copy.start()
    started.extend(copies_t)
    chips[number] = chip[...]

    received_g()
    grad = jnp.concatenate([halo_g[0], slab[NEAR : NEAR + BLK, :].astype(BF16), halo_g[1]], axis=0)
    blurred = [dot(tg[blk, :, 0:192], grad[:, blk * BLK : blk * BLK + BLK]) for blk in range(blocks)]
    spread = (twice(joined(blurred).astype(BF16)) * -STEP_SIZE).astype(BF16)
    conv_grad = conv_grad.astype(BF16)
    for blk in range(blocks):
        at = slice(blk * BLK, blk * BLK + BLK)
        change = tn_dot(spread[:, at], tt[blk, :, 0:BLK]) + tn_dot(conv_grad[:, at], eye)
        turned = tn_dot(conv_out[:, at], eye)
        for i in range(BLK // BAND):
            lines = slice(i * 8, i * 8 + 8)
            send_g[blk * (BLK // BAND) + i] = jnp.concatenate([turned[lines], change[lines]], axis=0).astype(BF16)
    copies_b = exchange(2, lambda to: send_g.at[to], back_g)
    back_g[me] = send_g[me]

    arrive(copies_t)
    total = chips[0].astype(F32)
    for i in range(1, n // 2):
        total = total + chips[i].astype(F32)
    whole[part(core), :] = total
    copy_w = to_pair(1, whole.at[part(core)], whole.at[part(core)])
    arrive(copies_b)
    for g in range(n):
        at = slice(g * BLK, g * BLK + BLK)
        back = back_g[g].astype(F32)
        den_ref[:, at] = est_ref[:, at] + back[0:8]
        ge_ref[:, at] = cot_in_ref[:, at] + back[8:16]
    copy_w.wait_recv()
    for slot in range(9):
        a, b = slot // 3, slot % 3
        gm_ref[slot] = whole[a * 32 : a * 32 + 32, b * 32 : b * 32 + 32]
        gf_ref[slot] = whole[3 * b + a : 3 * b + a + 1, 96:BLK]
        gl_ref[slot] = whole[9 + 3 * b + a : 10 + 3 * b + a, 96:BLK]
    sent_o()
    sent_g()
    for copy in started:
        copy.wait_send()


def deliver(*refs):
    sems = refs[-1]
    copies = [pltpu.make_async_copy(refs[i], refs[5 + i], sems.at[i]) for i in range(5)]
    for copy in copies:
        copy.start()
    for copy in copies:
        copy.wait()


def on_device(n, estimate, observed, cotangent, zone_map, bank_pick, psf_bank, w_first, w_mid, w_last):
    width = estimate.shape[1]
    height = BAND * n
    lanes = 2 * height
    blocks = height // BLK
    scale = GRAD_FACTOR / math.sqrt(height * width)
    vmem, hbm = pl.BlockSpec(memory_space=pltpu.VMEM), pl.BlockSpec(memory_space=pltpu.HBM)
    flat = pltpu.VMEM((n, 16, BLK), BF16)
    broad = pltpu.VMEM((n, 8, 4 * BLK), BF16)
    ends = jnp.transpose(w_first, (1, 2, 3, 0)), jnp.transpose(w_last, (0, 2, 3, 1))
    middle = jnp.transpose(w_mid, (2, 3, 0, 1)).reshape(9, CH, CH)
    operands = [
        pltpu.with_memory_space_constraint(v, pltpu.HBM)
        for v in (estimate, observed, cotangent, zone_map, bank_pick, psf_bank, *ends, middle)]
    results = pl.pallas_call(
        functools.partial(kernel, n, scale),
        out_shape=(
            pltpu.VMEM((8, width), F32),
            pltpu.VMEM((8, width), F32),
            pltpu.VMEM((9, CH, CH), F32),
            pltpu.VMEM((9, 1, CH), F32),
            pltpu.VMEM((9, 1, CH), F32),
        ),
        in_specs=[hbm] * 9,
        out_specs=[vmem] * 5,
        scratch_shapes=[
            pltpu.VMEM((8, width), F32),
            pltpu.VMEM((height, BLK), F32),
            pltpu.VMEM((8, width), F32),
            pltpu.SMEM(zone_map.shape, jnp.int32),
            pltpu.SMEM(bank_pick.shape, jnp.int32),
            pltpu.VMEM(psf_bank.shape, F32),
            pltpu.VMEM((1, 3, 3, CH), BF16),
            pltpu.VMEM((1, 3, 3, CH), BF16),
            pltpu.VMEM((9, CH, CH), BF16),
            pltpu.SemaphoreType.DMA((9,)),
            broad, broad, flat, flat,
            pltpu.VMEM((96, BLK), F32),
            pltpu.VMEM((48, BLK), F32),
            pltpu.VMEM((48, BLK), BF16),
            pltpu.VMEM((n // 2, 48, BLK), BF16),
            pltpu.VMEM((96, BLK), F32),
            pltpu.VMEM((2, EDGE, height), BF16),
            pltpu.VMEM((2, EDGE, height), BF16),
            pltpu.VMEM((2, NEAR, height), BF16),
            pltpu.VMEM((2, NEAR, height), BF16),
            pltpu.VMEM((blocks, WIDE, 256), BF16),
            pltpu.VMEM((blocks, 144, WIDE), BF16),
            pltpu.VMEM((blocks, WIDE, 256), BF16),
            pltpu.VMEM((3, height, height), BF16),
            pltpu.VMEM((144, height), F32),
            pltpu.VMEM((144, height), F32),
            pltpu.VMEM((144, height), F32),
            pltpu.VMEM((9, 48, lanes), BF16),
            pltpu.VMEM((12, 32, lanes), BF16),
            pltpu.VMEM((NEAR + BLK, height), F32),
            pltpu.VMEM((256, 48), BF16),
            pltpu.VMEM((192, 32), BF16),
            pltpu.VMEM((24, 320), BF16),
            pltpu.VMEM((24, 320), BF16),
            pltpu.VMEM((3, 192, 256), BF16),
            pltpu.VMEM((3, 192, 256), BF16),
            pltpu.VMEM((COLS_PRE * CH, lanes), BF16),
            pltpu.VMEM((3, COLS_PRE * CH, lanes), BF16),
            pltpu.VMEM((3, COLS_MID * CH, lanes), BF16),
            pltpu.VMEM((COLS_MID * CH, lanes), BF16),
            pltpu.VMEM((COLS_BACK * CH, lanes), BF16),
            pltpu.VMEM((8, 24, lanes), F32),
            pltpu.VMEM((3, 192, 256), F32),
            pltpu.VMEM((48, 256), F32),
            pltpu.SemaphoreType.DMA((3, n - 1)),
            pltpu.SemaphoreType.DMA((3, n - 1)),
            pltpu.SemaphoreType.DMA((3, 2)),
            pltpu.SemaphoreType.DMA((3, 2)),
        ],
        compiler_params=pltpu.CompilerParams(
            collective_id=0, has_side_effects=True, vmem_limit_bytes=40 << 20 if height <= 256 else 62 << 20),
    )(*operands)
    denoised, grad_estimate, grad_mid, grad_first, grad_last = pl.pallas_call(
        deliver,
        out_shape=tuple(pltpu.HBM(v.shape, v.dtype) for v in results),
        in_specs=[vmem] * 5,
        out_specs=[hbm] * 5,
        scratch_shapes=[pltpu.SemaphoreType.DMA((5,))],
    )(*[pltpu.with_memory_space_constraint(v, pltpu.VMEM) for v in results])
    grad_mid = jnp.transpose(grad_mid.reshape(3, 3, CH, CH), (2, 3, 0, 1))
    grad_first = jnp.transpose(grad_first.reshape(3, 3, 1, CH), (3, 2, 0, 1))
    grad_last = jnp.transpose(grad_last.reshape(3, 3, 1, CH), (2, 3, 0, 1))
    return denoised, grad_estimate, grad_first, grad_mid, grad_last


def solution(mesh):
    placed = (
        P(("parts", "rows"), None),
        P("parts", "rows"),
        P(("parts", "rows"), None),
        P("parts", None),
        P(), P(), P(), P(), P(),
    )
    return jax.shard_map(
        functools.partial(on_device, mesh.shape["rows"]),
        mesh=mesh,
        in_specs=placed,
        out_specs=(
            P(("parts", "rows"), None),
            P(("parts", "rows"), None),
            P("parts", None, None, None),
            P("parts", None, None, None),
            P("parts", None, None, None),
        ),
        check_vma=False,
    )
```

```python
import functools
import math

import jax
import jax.numpy as jnp
from jax import lax
from jax.experimental import pallas as pl
from jax.experimental.pallas import tpu as pltpu
from jax.sharding import PartitionSpec as P

BLK = 128
RAD = 12
TAPS = 2 * RAD + 1
CH = 32
BAND = 8
STEP_SIZE = 2.0
GRAD_FACTOR = 8.0
MESH = pl.DeviceIdType.MESH
F32 = jnp.float32
BF16 = jnp.bfloat16

EDGE = 16
WIDE = BLK + 2 * EDGE
NEAR = 32
COLS_PRE, COLS_MID, COLS_BACK = 70, 68, 66


def tn_dot(a, b, **kw):
    return lax.dot_general(a, b, (((0,), (0,)), ((), ())), preferred_element_type=F32, **kw)


def nt_dot(a, b):
    return lax.dot_general(a, b, (((1,), (1,)), ((), ())), preferred_element_type=F32)


def dot(a, b, **kw):
    return jnp.dot(a, b, preferred_element_type=F32, **kw)


def iota(shape, dim):
    return lax.broadcasted_iota(jnp.int32, shape, dim)


def third(v, size):
    return (v >= size).astype(jnp.int32) + (v >= 2 * size).astype(jnp.int32)


def ones_where(cond):
    return jnp.where(cond, 1.0, 0.0).astype(BF16)


def silu_pair_of_half(h):
    t = jnp.tanh(h)
    q = 0.5 * t
    act = h + h * t
    return act, (0.5 + q) + act * (0.5 - q)


def moved(v, delta, height):
    parts = []
    for at in range(0, v.shape[1], height):
        part = v[:, at : at + height]
        lane = iota((1, height), 1)
        edge = height - 1 if delta == 1 else 0
        keep = jnp.where(lane == edge, 0.0, 1.0).astype(v.dtype)
        parts.append(pltpu.roll(part, height - 1 if delta == 1 else 1, 1) * keep)
    return jnp.concatenate(parts, axis=1)


def build_weights(wf_ref, wl_ref, w9_ref, w1, wlt, wl3, wf3, wmb, wmtb):
    wf, wl = [
        jnp.concatenate([ref[0, a].astype(F32) for a in range(3)], axis=0).astype(BF16) for ref in (wf_ref, wl_ref)]

    def taps(shape, dim):
        k = iota(shape, dim)
        ka = third(k, 3)
        return ka, k - 3 * ka

    ka, kb = taps((9, 48), 0)
    lane = iota((9, 48), 1)
    la = third(lane, 16)
    lc = lane - 16 * la
    for r in range(8):
        pick = ones_where(jnp.logical_and(ka == la, kb == lc - r)) * 0.5
        w1[r * 32 : r * 32 + 32, :] = tn_dot(wf, pick.astype(BF16)).astype(BF16)
    ka, kb = taps((9, 32), 0)
    lane = iota((9, 32), 1)
    la = third(lane, 8)
    lc = lane - 8 * la
    for r in range(6):
        pick = ones_where(jnp.logical_and(jnp.logical_and(ka == la, lane < 24), kb == r + 2 - lc))
        wlt[r * 32 : r * 32 + 32, :] = tn_dot(wl, pick).astype(BF16)
    ka, kb = taps((24, 9), 1)
    out = iota((24, 9), 0)
    oa = third(out, 8)
    orow = out - 8 * oa
    for q in range(10):
        fwd = ones_where(jnp.logical_and(ka == oa, kb == q - orow))
        wl3[:, q * 32 : q * 32 + 32] = dot(fwd, wl).astype(BF16)
        adj = ones_where(jnp.logical_and(ka == oa, kb == orow + 2 - q))
        wf3[:, q * 32 : q * 32 + 32] = dot(adj, wf).astype(BF16)
    eye = ones_where(iota((32, 32), 0) == iota((32, 32), 1))
    wmb[...] = jnp.zeros_like(wmb)
    wmtb[...] = jnp.zeros_like(wmtb)
    for a in range(3):
        line = jnp.concatenate([w9_ref[a * 3 + b] for b in range(3)], axis=1)
        line = (line.astype(F32) * 0.5).astype(BF16)
        turned = [nt_dot(eye, w9_ref[a * 3 + 2 - q]) for q in range(3)]
        turned = jnp.concatenate(turned, axis=1).astype(BF16)
        for r in range(6):
            wmb[a, r * 32 : r * 32 + 32, r * 32 : r * 32 + 96] = line
            wmtb[a, r * 32 : r * 32 + 32, r * 32 : r * 32 + 96] = turned


def kernel(
    n, scale,
    est_hbm, obs_hbm, cot_hbm, zone_hbm, pick_hbm, psf_hbm, wf_hbm, wl_hbm, w9_hbm,
    den_ref, ge_ref, gm_ref, gf_ref, gl_ref,
    est_ref, obs_ref, cot_in_ref, zone_ref, pick_ref, psf_ref, wf_ref, wl_ref, w9_ref, load_sems,
    send_e, recv_e, send_g, back_g,
    share, share_in, chip, chips, whole,
    strip, halo, strip_g, halo_g,
    tt, t2, tg, mats, ds_ref, rp_ref, cot_ref, fw, cw, slab,
    w1, wlt, wl3, wf3, wmb, wmtb, slope1, x3, x3b, mid, bfr, d24, gm_acc, gf_acc,
    send_sems, recv_sems, hs, hr,
):
    me = lax.axis_index("rows")
    height = BAND * n
    blocks = height // BLK
    width = BLK * n
    lanes = 2 * height
    first, last = me == 0, me == n - 1
    started = []

    def peer(k):
        return lax.rem(me + k, n)

    loads = []
    for i, (src, dst) in enumerate((
            (est_hbm, est_ref), (cot_hbm, cot_in_ref), (zone_hbm, zone_ref), (pick_hbm, pick_ref), (psf_hbm, psf_ref),
            (obs_hbm, obs_ref), (wf_hbm, wf_ref), (wl_hbm, wl_ref), (w9_hbm, w9_ref))):
        loads.append(pltpu.make_async_copy(src, dst, load_sems.at[i]))
        loads[-1].start()

    barrier = pltpu.get_barrier_semaphore()
    for k in range(1, n):
        pl.semaphore_signal(barrier, inc=1, device_id={"rows": peer(k)}, device_id_type=MESH)

    def exchange(index, src_at, dst):
        copies = []
        for k in range(1, n):
            to = peer(k)
            copies.append(pltpu.make_async_remote_copy(
                src_ref=src_at(to), dst_ref=dst.at[me],
                send_sem=send_sems.at[index, k - 1], recv_sem=recv_sems.at[index, k - 1],
                device_id={"rows": to}, device_id_type=MESH))
        for copy in copies:
            copy.start()
        started.extend(copies)
        return copies

    def neighbours(index, src, dst):
        copies = []
        for side, k in ((0, 1), (1, n - 1)):
            copies.append(pltpu.make_async_remote_copy(
                src_ref=src.at[side], dst_ref=dst.at[side],
                send_sem=hs.at[index, side], recv_sem=hr.at[index, side],
                device_id={"rows": peer(k)}, device_id_type=MESH))
        for copy in copies:
            copy.start()
        started.extend(copies)
        return copies

    def arrive(copies):
        for copy in copies:
            copy.wait_recv()

    for copy in loads[0:2]:
        copy.wait()
    lane = iota((BAND, BLK), 1)
    zero = jnp.zeros((BAND, BLK), F32)
    hi, lo, ct = [zero], [zero], [zero]
    for g in range(n):
        own = est_ref[:, g * BLK : g * BLK + BLK]
        hi.append(own.astype(BF16).astype(F32))
        lo.append(own - hi[-1])
        ct.append(cot_in_ref[:, g * BLK : g * BLK + BLK])
    hi, lo, ct = hi + [zero], lo + [zero], ct + [zero]
    for g in range(n):
        p, c, q = g, g + 1, g + 2
        around = jnp.where(lane < 64, hi[q], hi[p])
        around = jnp.where(jnp.logical_and(lane >= 32, lane < 96), jnp.where(
            lane < 64, pltpu.roll(lo[q], 32, 1), pltpu.roll(lo[p], BLK - 32, 1)), around)
        around = jnp.where(jnp.logical_and(lane >= 40, lane < 88), jnp.where(
            lane < 64, pltpu.roll(ct[q], 40, 1), pltpu.roll(ct[p], BLK - 40, 1)), around)
        send_e[g] = jnp.concatenate([hi[c], around, lo[c], ct[c]], axis=1).astype(BF16)
    pl.semaphore_wait(barrier, n - 1)
    copies_e = exchange(0, lambda to: send_e.at[to], recv_e)
    recv_e[me] = send_e[me]
    for copy in loads[2:]:
        copy.wait()

    psf = psf_ref[...]
    norm = psf / jnp.sum(psf, axis=1, keepdims=True)
    bank = iota((8, TAPS), 0)
    left, right = jnp.maximum(me - 1, 0), jnp.minimum(me + 1, n - 1)

    def taps_of(which, blk, group):
        k = pick_ref[which, zone_ref[blk, group]]
        return jnp.sum(jnp.where(bank == k, norm, 0.0), axis=0, keepdims=True)

    def banded(parts, wide, at):
        ahead = at % 8
        lines = []
        for taps, count in parts:
            line = [taps, jnp.zeros((1, wide - TAPS - ahead), F32)]
            line = jnp.concatenate([jnp.zeros((1, ahead), F32)] * (ahead > 0) + line, axis=1)
            lines.append(jnp.broadcast_to(line, (count, wide)))
        lines = lines[0] if len(lines) == 1 else jnp.concatenate(lines, axis=0)
        return pltpu.roll(lines, (at - ahead) % wide, 1, stride=1, stride_axis=0)

    for blk in range(blocks):
        parts = [
            (jnp.where(first, 0.0, taps_of(0, blk, left)), EDGE), (taps_of(0, blk, me), BLK),
            (jnp.where(last, 0.0, taps_of(0, blk, right)), EDGE)]
        tt[blk] = banded(parts, 256, -28).astype(BF16)
        turned = jnp.concatenate([banded(parts, 256, -24), jnp.zeros((256 - WIDE, 256), F32)], axis=0).T
        t2[blk] = (turned[0:144, 0:WIDE] * -STEP_SIZE).astype(BF16)
        lane = iota((WIDE, 256), 1)
        gone = jnp.logical_or(jnp.logical_and(lane < NEAR, first), jnp.logical_and(lane >= NEAR + BLK, last))
        tg[blk] = jnp.where(gone, 0.0, banded(parts, 256, 4)).astype(BF16)

    def column_operator(group):
        parts = [(taps_of(1, blk, group), BLK) for blk in range(blocks)]
        return banded(parts, height + BLK, -RAD)[:, 0:height]

    own = column_operator(me)
    target = tn_dot(obs_ref[...].astype(BF16), own.astype(BF16))
    strip[0] = target[BLK - EDGE : BLK, :].astype(BF16)
    strip[1] = target[0:EDGE, :].astype(BF16)
    copies_o = neighbours(0, strip, halo)
    slab[0:BLK, :] = target
    for i, op in enumerate((column_operator(left), own, column_operator(right))):
        mats[i] = tn_dot(op, op, precision=lax.Precision.HIGHEST).astype(BF16)
    build_weights(wf_ref, wl_ref, w9_ref, w1, wlt, wl3, wf3, wmb, wmtb)
    row, lane = iota((144, 384), 0), iota((144, 384), 1)
    rest = jnp.where(row < 4, row + 220, jnp.where(row < 132, row + 252, row + 28))
    sel = ones_where(jnp.logical_or(jnp.bitwise_and(row - 4, 255) == lane, rest == lane))
    row, lane = iota((144, 256), 0), iota((144, 256), 1)
    sel_c = ones_where(jnp.where(row < 4, row + 212, jnp.where(row < 132, row - 4, row + 36)) == lane)
    eye = ones_where(iota((BLK, BLK), 0) == iota((BLK, BLK), 1))

    def twice(v):
        return jnp.concatenate(
            [dot(v[0:EDGE], mats[0]), dot(v[EDGE : EDGE + BLK], mats[1]), dot(v[EDGE + BLK : WIDE], mats[2])], axis=0)

    def gather(blk):
        per = BLK // BAND
        return jnp.concatenate([recv_e[blk * per + i].astype(F32) for i in range(per)], axis=0).astype(BF16)

    def joined(parts):
        return parts[0] if len(parts) == 1 else jnp.concatenate(parts, axis=1)

    def halves(v):
        low = jnp.concatenate([v[0:72], v[64:136]], axis=1)
        return jnp.concatenate([low, jnp.zeros((8, lanes), F32)], axis=0)

    arrive(copies_e)
    est = [gather(blk) for blk in range(blocks)]
    blurred = joined([nt_dot(tt[blk], est[blk][:, 0:256]) for blk in range(blocks)]).astype(BF16)
    arrive(copies_o)
    target = jnp.concatenate([halo[0].astype(F32), slab[0:BLK, :], halo[1].astype(F32)], axis=0)
    spread = (twice(blurred) - target).astype(BF16)
    row = iota((144, height), 0)
    outside = jnp.logical_or(jnp.logical_and(row < 4, first), jnp.logical_and(row >= 4 + BLK, last))
    change = joined([dot(t2[blk], spread[:, blk * BLK : blk * BLK + BLK]) for blk in range(blocks)])
    rp_ref[...] = change
    ds = joined([nt_dot(sel, est[blk][:, 0:384]) for blk in range(blocks)]) + change
    ds = halves(jnp.where(outside, 0.0, ds))
    for a in range(3):
        line = ds if a == 1 else moved(ds, a - 1, height)
        for w in range(9):
            fw[w, a * 16 : a * 16 + 16, :] = line[8 * w : 8 * w + 16].astype(BF16)

    cot = joined([
        nt_dot(sel_c, jnp.concatenate([est[blk][:, 3 * BLK :], est[blk][:, BLK : 2 * BLK]], axis=1))
        for blk in range(blocks)])
    cot_ref[...] = cot
    cot = halves(cot)
    lines = [moved(cot, 1, height), cot, moved(cot, -1, height)]
    pad = jnp.zeros((8, lanes), F32)
    for w in range(12):
        at = 6 * w + 1
        cw[w] = jnp.concatenate([line[at : at + 8] for line in lines] + [pad], axis=0).astype(BF16)

    half = iota((1, lanes), 1) >= height

    def masked(v, start, begin, end):
        col = iota(v.shape, 0) // CH + start
        gone = jnp.logical_or(
            jnp.logical_and(jnp.logical_and(col < begin, first), jnp.logical_not(half)),
            jnp.logical_and(jnp.logical_and(col >= end, last), half))
        return jnp.where(gone, 0.0, v)

    def rows(at, count):
        return pl.ds(at if isinstance(at, int) else pl.multiple_of(at, 64), count)

    def conv_first(w, cols, edge):
        size = cols * CH
        act, slope = silu_pair_of_half(dot(w1[0:size, :], fw[w]))
        if edge:
            act = masked(act, 8 * w, 3, COLS_PRE - 3)
        act = act.astype(BF16)
        at = rows(w * 256, size)
        slope1[at, :] = slope.astype(BF16)
        x3[0, at, :] = moved(act, -1, height)
        x3[1, at, :] = act
        x3[2, at, :] = moved(act, 1, height)

    def run(body, count, tail):
        body(0, tail[0], True)
        if blocks == 1:
            for w in range(1, count - 1):
                body(w, tail[0], False)
        else:
            @pl.loop(1, count - 1)
            def _(w):
                body(w, tail[0], False)
        body(count - 1, tail[1], True)

    run(conv_first, 9, (8, 6))

    def conv_mid(w, cols, edge):
        size, deep = cols * CH, (cols + 2) * CH
        at = rows(w * 192, size)
        total = dot(wmb[0, 0:size, 0:deep], x3[0, rows(w * 192, deep), :])
        for a in (1, 2):
            total = total + dot(wmb[a, 0:size, 0:deep], x3[a, rows(w * 192, deep), :])
        act, slope = silu_pair_of_half(total)
        back = dot(wlt[0:size, :], cw[w]) * slope
        if edge:
            act = masked(act, 6 * w, 2, COLS_MID - 2)
            back = masked(back, 6 * w, 2, COLS_MID - 2)
        mid[at, :] = act.astype(BF16)
        back = back.astype(BF16)
        x3b[0, at, :] = moved(back, 1, height)
        x3b[1, at, :] = back
        x3b[2, at, :] = moved(back, -1, height)

    run(conv_mid, 12, (6, 2))

    def conv_back(w, cols, edge):
        size, deep = cols * CH, (cols + 2) * CH
        total = dot(wmtb[0, 0:size, 0:deep], x3b[0, rows(w * 192, deep), :])
        for a in (1, 2):
            total = total + dot(wmtb[a, 0:size, 0:deep], x3b[a, rows(w * 192, deep), :])
        total = total * slope1[rows(w * 192 + 64, size), :].astype(F32)
        if edge:
            total = masked(total, 6 * w, 1, COLS_BACK - 1)
        bfr[rows(w * 192, size), :] = total.astype(BF16)

    run(conv_back, 11, (6, 6))

    def assembled(sign):
        low, at, high = [jnp.concatenate([d24[w, a * 8 : a * 8 + 8, :] for w in range(8)], axis=0) for a in range(3)]
        total = at + moved(low, -sign, height) + moved(high, sign, height)
        return jnp.concatenate([total[:, 0:height], total[:, height:lanes]], axis=0)

    for w in range(8):
        d24[w] = dot(wf3[...], bfr[w * 256 : w * 256 + 320, :])
    conv_grad = assembled(-1)
    slab[NEAR : NEAR + BLK, :] = conv_grad + cot_ref[4 : 4 + BLK, :]
    strip_g[0] = slab[BLK : BLK + NEAR, :].astype(BF16)
    strip_g[1] = slab[NEAR : 2 * NEAR, :].astype(BF16)
    copies_g = neighbours(1, strip_g, halo_g)

    def beside(parts):
        return jnp.concatenate(parts, axis=1)

    def last_dot():
        lines = []
        for w in range(11):
            line = cw[w]
            if w in (0, 10):
                drop = 2 if w == 0 else 7
                r = iota((32, 1), 0)
                skip = jnp.logical_or(r == drop, jnp.logical_or(r == drop + 8, r == drop + 16))
                line = line * jnp.where(skip, 0.0, 1.0).astype(BF16)
            lines.append(line)
        return nt_dot(beside(lines), beside([mid[w * 192 : w * 192 + 256, :] for w in range(11)]))

    def first_dot():
        gf_acc[...] = jnp.where(iota((48, 256), 1) >= CH, nt_dot(fw[0], bfr[0:256, :]), 0.0) + nt_dot(
            beside([fw[w] for w in range(1, 8)]), beside([bfr[w * 256 : w * 256 + 256, :] for w in range(1, 8)]))
        gf_acc[:, 0:CH] += nt_dot(fw[8], bfr[2048 : 2048 + CH, :])
        return gf_acc[...]

    per = 10 if blocks == 1 else 2
    for g in range(0, 10, per):
        acts = beside([x3[1, w * 192 + 64 : w * 192 + 320, :] for w in range(g, g + per)])
        backs = beside([x3b[:, w * 192 + 64 : w * 192 + 256, :].reshape(576, lanes) for w in range(g, g + per)])
        total = nt_dot(backs, acts).reshape(3, 192, 256)
        gm_acc[...] = total if g == 0 else gm_acc[...] + total
    gm_acc[:, 0:128, 0:192] += nt_dot(
        x3b[:, 62 * CH : 66 * CH, :].reshape(384, lanes), x3[1, 62 * CH : 68 * CH, :]).reshape(3, 128, 192)

    for a in range(3):
        total = gm_acc[a, 0:32, :]
        for r in range(1, 6):
            total = total + pltpu.roll(gm_acc[a, r * 32 : r * 32 + 32, :], 256 - 32 * r, 1)
        share[a * 32 : a * 32 + 32, :] = total[:, 0:BLK] * scale
    ends = []
    for acc, deep, ahead in ((first_dot(), 16, 2), (last_dot(), 8, 2)):
        acc = acc[0 : 3 * deep].reshape(3, deep, 256)
        c, col = iota((3, deep, 256), 1), iota((3, deep, 256), 2) // CH
        for b in range(3):
            hit = c == col + 2 + b if deep == 16 else jnp.logical_and(c >= 2, c - 2 + b == col)
            ends.append(jnp.sum(jnp.where(hit, acc, 0.0), axis=1))
    ends = jnp.concatenate(ends + [jnp.zeros((6, 256), F32)], axis=0)
    ends = ends[:, 0:BLK] + ends[:, BLK:]
    ends = ends + pltpu.roll(ends, 64, 1)
    ends = (ends + pltpu.roll(ends, 32, 1)) * scale
    share[0:24, 96:BLK] = ends[:, 96:BLK]

    core = lax.rem(me, 2)
    pair = me + 1 - 2 * core

    def part(i):
        return pl.ds(pl.multiple_of(i * 48, 16), 48)

    def to_pair(index, src, dst):
        copy = pltpu.make_async_remote_copy(
            src_ref=src, dst_ref=dst, send_sem=hs.at[2, index], recv_sem=hr.at[2, index],
            device_id={"rows": pair}, device_id_type=MESH)
        copy.start()
        started.append(copy)
        return copy

    copy_s = to_pair(0, share.at[part(1 - core)], share_in)

    for w in range(8):
        d24[w] = dot(wl3[...], mid[w * 256 + 32 : w * 256 + 352, :])
    conv_out = (rp_ref[4 : 4 + BLK, :] + assembled(1)).astype(BF16)
    copy_s.wait_recv()
    number = me // 2
    chip[...] = (share[part(core), :] + share_in[...]).astype(BF16)
    copies_t = []
    for k in range(1, n // 2):
        copies_t.append(pltpu.make_async_remote_copy(
            src_ref=chip, dst_ref=chips.at[number],
            send_sem=send_sems.at[1, k - 1], recv_sem=recv_sems.at[1, k - 1],
            device_id={"rows": lax.rem(me + 2 * k, n)}, device_id_type=MESH))
    for copy in copies_t:
        copy.start()
    started.extend(copies_t)
    chips[number] = chip[...]

    arrive(copies_g)
    grad = jnp.concatenate([halo_g[0], slab[NEAR : NEAR + BLK, :].astype(BF16), halo_g[1]], axis=0)
    blurred = [dot(tg[blk, :, 0:192], grad[:, blk * BLK : blk * BLK + BLK]) for blk in range(blocks)]
    spread = (twice(joined(blurred).astype(BF16)) * -STEP_SIZE).astype(BF16)
    conv_grad = conv_grad.astype(BF16)
    for blk in range(blocks):
        at = slice(blk * BLK, blk * BLK + BLK)
        change = tn_dot(spread[:, at], tt[blk, :, 0:BLK]) + tn_dot(conv_grad[:, at], eye)
        turned = tn_dot(conv_out[:, at], eye)
        for i in range(BLK // BAND):
            lines = slice(i * 8, i * 8 + 8)
            send_g[blk * (BLK // BAND) + i] = jnp.concatenate([turned[lines], change[lines]], axis=0).astype(BF16)
    copies_b = exchange(2, lambda to: send_g.at[to], back_g)
    back_g[me] = send_g[me]

    arrive(copies_t)
    total = chips[0].astype(F32)
    for i in range(1, n // 2):
        total = total + chips[i].astype(F32)
    whole[part(core), :] = total
    copy_w = to_pair(1, whole.at[part(core)], whole.at[part(core)])
    arrive(copies_b)
    for g in range(n):
        at = slice(g * BLK, g * BLK + BLK)
        back = back_g[g].astype(F32)
        den_ref[:, at] = est_ref[:, at] + back[0:8]
        ge_ref[:, at] = cot_in_ref[:, at] + back[8:16]
    copy_w.wait_recv()
    for slot in range(9):
        a, b = slot // 3, slot % 3
        gm_ref[slot] = whole[a * 32 : a * 32 + 32, b * 32 : b * 32 + 32]
        gf_ref[slot] = whole[3 * b + a : 3 * b + a + 1, 96:BLK]
        gl_ref[slot] = whole[9 + 3 * b + a : 10 + 3 * b + a, 96:BLK]
    for copy in started:
        copy.wait_send()


def deliver(*refs):
    sems = refs[-1]
    copies = [pltpu.make_async_copy(refs[i], refs[5 + i], sems.at[i]) for i in range(5)]
    for copy in copies:
        copy.start()
    for copy in copies:
        copy.wait()


def on_device(n, estimate, observed, cotangent, zone_map, bank_pick, psf_bank, w_first, w_mid, w_last):
    width = estimate.shape[1]
    height = BAND * n
    lanes = 2 * height
    blocks = height // BLK
    scale = GRAD_FACTOR / math.sqrt(height * width)
    vmem, hbm = pl.BlockSpec(memory_space=pltpu.VMEM), pl.BlockSpec(memory_space=pltpu.HBM)
    flat = pltpu.VMEM((n, 16, BLK), BF16)
    broad = pltpu.VMEM((n, 8, 4 * BLK), BF16)
    ends = jnp.transpose(w_first, (1, 2, 3, 0)), jnp.transpose(w_last, (0, 2, 3, 1))
    middle = jnp.transpose(w_mid, (2, 3, 0, 1)).reshape(9, CH, CH)
    operands = [
        pltpu.with_memory_space_constraint(v, pltpu.HBM)
        for v in (estimate, observed, cotangent, zone_map, bank_pick, psf_bank, *ends, middle)]
    results = pl.pallas_call(
        functools.partial(kernel, n, scale),
        out_shape=(
            pltpu.VMEM((8, width), F32),
            pltpu.VMEM((8, width), F32),
            pltpu.VMEM((9, CH, CH), F32),
            pltpu.VMEM((9, 1, CH), F32),
            pltpu.VMEM((9, 1, CH), F32),
        ),
        in_specs=[hbm] * 9,
        out_specs=[vmem] * 5,
        scratch_shapes=[
            pltpu.VMEM((8, width), F32),
            pltpu.VMEM((height, BLK), F32),
            pltpu.VMEM((8, width), F32),
            pltpu.SMEM(zone_map.shape, jnp.int32),
            pltpu.SMEM(bank_pick.shape, jnp.int32),
            pltpu.VMEM(psf_bank.shape, F32),
            pltpu.VMEM((1, 3, 3, CH), BF16),
            pltpu.VMEM((1, 3, 3, CH), BF16),
            pltpu.VMEM((9, CH, CH), BF16),
            pltpu.SemaphoreType.DMA((9,)),
            broad, broad, flat, flat,
            pltpu.VMEM((96, BLK), F32),
            pltpu.VMEM((48, BLK), F32),
            pltpu.VMEM((48, BLK), BF16),
            pltpu.VMEM((n // 2, 48, BLK), BF16),
            pltpu.VMEM((96, BLK), F32),
            pltpu.VMEM((2, EDGE, height), BF16),
            pltpu.VMEM((2, EDGE, height), BF16),
            pltpu.VMEM((2, NEAR, height), BF16),
            pltpu.VMEM((2, NEAR, height), BF16),
            pltpu.VMEM((blocks, WIDE, 256), BF16),
            pltpu.VMEM((blocks, 144, WIDE), BF16),
            pltpu.VMEM((blocks, WIDE, 256), BF16),
            pltpu.VMEM((3, height, height), BF16),
            pltpu.VMEM((144, height), F32),
            pltpu.VMEM((144, height), F32),
            pltpu.VMEM((144, height), F32),
            pltpu.VMEM((9, 48, lanes), BF16),
            pltpu.VMEM((12, 32, lanes), BF16),
            pltpu.VMEM((NEAR + BLK, height), F32),
            pltpu.VMEM((256, 48), BF16),
            pltpu.VMEM((192, 32), BF16),
            pltpu.VMEM((24, 320), BF16),
            pltpu.VMEM((24, 320), BF16),
            pltpu.VMEM((3, 192, 256), BF16),
            pltpu.VMEM((3, 192, 256), BF16),
            pltpu.VMEM((COLS_PRE * CH, lanes), BF16),
            pltpu.VMEM((3, COLS_PRE * CH, lanes), BF16),
            pltpu.VMEM((3, COLS_MID * CH, lanes), BF16),
            pltpu.VMEM((COLS_MID * CH, lanes), BF16),
            pltpu.VMEM((COLS_BACK * CH, lanes), BF16),
            pltpu.VMEM((8, 24, lanes), F32),
            pltpu.VMEM((3, 192, 256), F32),
            pltpu.VMEM((48, 256), F32),
            pltpu.SemaphoreType.DMA((3, n - 1)),
            pltpu.SemaphoreType.DMA((3, n - 1)),
            pltpu.SemaphoreType.DMA((3, 2)),
            pltpu.SemaphoreType.DMA((3, 2)),
        ],
        compiler_params=pltpu.CompilerParams(
            collective_id=0, has_side_effects=True, vmem_limit_bytes=40 << 20 if height <= 256 else 62 << 20),
    )(*operands)
    denoised, grad_estimate, grad_mid, grad_first, grad_last = pl.pallas_call(
        deliver,
        out_shape=tuple(pltpu.HBM(v.shape, v.dtype) for v in results),
        in_specs=[vmem] * 5,
        out_specs=[hbm] * 5,
        scratch_shapes=[pltpu.SemaphoreType.DMA((5,))],
    )(*[pltpu.with_memory_space_constraint(v, pltpu.VMEM) for v in results])
    grad_mid = jnp.transpose(grad_mid.reshape(3, 3, CH, CH), (2, 3, 0, 1))
    grad_first = jnp.transpose(grad_first.reshape(3, 3, 1, CH), (3, 2, 0, 1))
    grad_last = jnp.transpose(grad_last.reshape(3, 3, 1, CH), (2, 3, 0, 1))
    return denoised, grad_estimate, grad_first, grad_mid, grad_last


def solution(mesh):
    placed = (
        P(("parts", "rows"), None),
        P("parts", "rows"),
        P(("parts", "rows"), None),
        P("parts", None),
        P(), P(), P(), P(), P(),
    )
    return jax.shard_map(
        functools.partial(on_device, mesh.shape["rows"]),
        mesh=mesh,
        in_specs=placed,
        out_specs=(
            P(("parts", "rows"), None),
            P(("parts", "rows"), None),
            P("parts", None, None, None),
            P("parts", None, None, None),
            P("parts", None, None, None),
        ),
        check_vma=False,
    )
```

```python
import functools
import math

import jax
import jax.numpy as jnp
from jax import lax
from jax.experimental import pallas as pl
from jax.experimental.pallas import tpu as pltpu
from jax.sharding import PartitionSpec as P

BLK = 128
RAD = 12
TAPS = 2 * RAD + 1
CH = 32
BAND = 8
STEP_SIZE = 2.0
GRAD_FACTOR = 8.0
MESH = pl.DeviceIdType.MESH
F32 = jnp.float32
BF16 = jnp.bfloat16

EDGE = 16
WIDE = BLK + 2 * EDGE
NEAR = 32
COLS_PRE, COLS_MID, COLS_BACK = 70, 68, 66


def tn_dot(a, b, **kw):
    return lax.dot_general(a, b, (((0,), (0,)), ((), ())), preferred_element_type=F32, **kw)


def nt_dot(a, b):
    return lax.dot_general(a, b, (((1,), (1,)), ((), ())), preferred_element_type=F32)


def dot(a, b, **kw):
    return jnp.dot(a, b, preferred_element_type=F32, **kw)


def iota(shape, dim):
    return lax.broadcasted_iota(jnp.int32, shape, dim)


def third(v, size):
    return (v >= size).astype(jnp.int32) + (v >= 2 * size).astype(jnp.int32)


def ones_where(cond):
    return jnp.where(cond, 1.0, 0.0).astype(BF16)


def silu_pair_of_half(h):
    t = jnp.tanh(h)
    q = 0.5 * t
    act = h + h * t
    return act, (0.5 + q) + act * (0.5 - q)


def moved(v, delta, height):
    parts = []
    for at in range(0, v.shape[1], height):
        part = v[:, at : at + height]
        lane = iota((1, height), 1)
        edge = height - 1 if delta == 1 else 0
        keep = jnp.where(lane == edge, 0.0, 1.0).astype(v.dtype)
        parts.append(pltpu.roll(part, height - 1 if delta == 1 else 1, 1) * keep)
    return jnp.concatenate(parts, axis=1)


def build_weights(wf_ref, wl_ref, w9_ref, w1, wlt, wl3, wf3, wmb, wmtb):
    wf, wl = [
        jnp.concatenate([ref[0, a].astype(F32) for a in range(3)], axis=0).astype(BF16) for ref in (wf_ref, wl_ref)]

    def taps(shape, dim):
        k = iota(shape, dim)
        ka = third(k, 3)
        return ka, k - 3 * ka

    ka, kb = taps((9, 48), 0)
    lane = iota((9, 48), 1)
    la = third(lane, 16)
    lc = lane - 16 * la
    for r in range(8):
        pick = ones_where(jnp.logical_and(ka == la, kb == lc - r)) * 0.5
        w1[r * 32 : r * 32 + 32, :] = tn_dot(wf, pick.astype(BF16)).astype(BF16)
    ka, kb = taps((9, 32), 0)
    lane = iota((9, 32), 1)
    la = third(lane, 8)
    lc = lane - 8 * la
    for r in range(6):
        pick = ones_where(jnp.logical_and(jnp.logical_and(ka == la, lane < 24), kb == r + 2 - lc))
        wlt[r * 32 : r * 32 + 32, :] = tn_dot(wl, pick).astype(BF16)
    ka, kb = taps((24, 9), 1)
    out = iota((24, 9), 0)
    oa = third(out, 8)
    orow = out - 8 * oa
    for q in range(10):
        fwd = ones_where(jnp.logical_and(ka == oa, kb == q - orow))
        wl3[:, q * 32 : q * 32 + 32] = dot(fwd, wl).astype(BF16)
        adj = ones_where(jnp.logical_and(ka == oa, kb == orow + 2 - q))
        wf3[:, q * 32 : q * 32 + 32] = dot(adj, wf).astype(BF16)
    eye = ones_where(iota((32, 32), 0) == iota((32, 32), 1))
    wmb[...] = jnp.zeros_like(wmb)
    wmtb[...] = jnp.zeros_like(wmtb)
    for a in range(3):
        line = jnp.concatenate([w9_ref[a * 3 + b] for b in range(3)], axis=1)
        line = (line.astype(F32) * 0.5).astype(BF16)
        turned = [nt_dot(eye, w9_ref[a * 3 + 2 - q]) for q in range(3)]
        turned = jnp.concatenate(turned, axis=1).astype(BF16)
        for r in range(6):
            wmb[a, r * 32 : r * 32 + 32, r * 32 : r * 32 + 96] = line
            wmtb[a, r * 32 : r * 32 + 32, r * 32 : r * 32 + 96] = turned


def kernel(
    n, scale,
    est_hbm, obs_hbm, cot_hbm, zone_hbm, pick_hbm, psf_hbm, wf_hbm, wl_hbm, w9_hbm,
    den_ref, ge_ref, gm_ref, gf_ref, gl_ref,
    est_ref, obs_ref, cot_in_ref, zone_ref, pick_ref, psf_ref, wf_ref, wl_ref, w9_ref, load_sems,
    send_e, recv_e, send_g, back_g,
    share, share_in, chip, chips, whole,
    strip, halo, strip_g, halo_g,
    tt, t2, tg, mats, ds_ref, rp_ref, cot_ref, fw, cw, slab,
    w1, wlt, wl3, wf3, wmb, wmtb, slope1, x3, x3b, mid, bfr, d24, gm_acc, gf_acc,
    send_sems, recv_sems, hs, hr,
):
    me = lax.axis_index("rows")
    height = BAND * n
    blocks = height // BLK
    width = BLK * n
    lanes = 2 * height
    first, last = me == 0, me == n - 1
    started = []

    def peer(k):
        return lax.rem(me + k, n)

    loads = []
    for i, (src, dst) in enumerate((
            (est_hbm, est_ref), (cot_hbm, cot_in_ref), (zone_hbm, zone_ref), (pick_hbm, pick_ref), (psf_hbm, psf_ref),
            (obs_hbm, obs_ref), (wf_hbm, wf_ref), (wl_hbm, wl_ref), (w9_hbm, w9_ref))):
        loads.append(pltpu.make_async_copy(src, dst, load_sems.at[i]))
        loads[-1].start()

    barrier = pltpu.get_barrier_semaphore()
    for k in range(1, n):
        pl.semaphore_signal(barrier, inc=1, device_id={"rows": peer(k)}, device_id_type=MESH)

    def exchange(index, src_at, dst):
        copies = []
        for k in range(1, n):
            to = peer(k)
            copies.append(pltpu.make_async_remote_copy(
                src_ref=src_at(to), dst_ref=dst.at[me],
                send_sem=send_sems.at[index, k - 1], recv_sem=recv_sems.at[index, k - 1],
                device_id={"rows": to}, device_id_type=MESH))
        for copy in copies:
            copy.start()
        started.extend(copies)
        return copies

    def neighbours(index, src, dst):
        copies = []
        for side, k in ((0, 1), (1, n - 1)):
            copies.append(pltpu.make_async_remote_copy(
                src_ref=src.at[side], dst_ref=dst.at[side],
                send_sem=hs.at[index, side], recv_sem=hr.at[index, side],
                device_id={"rows": peer(k)}, device_id_type=MESH))
        for copy in copies:
            copy.start()
        started.extend(copies)
        return copies

    def arrive(copies):
        for copy in copies:
            copy.wait_recv()

    for copy in loads[0:2]:
        copy.wait()
    lane = iota((BAND, BLK), 1)
    zero = jnp.zeros((BAND, BLK), F32)
    hi, lo, ct = [zero], [zero], [zero]
    for g in range(n):
        own = est_ref[:, g * BLK : g * BLK + BLK]
        hi.append(own.astype(BF16).astype(F32))
        lo.append(own - hi[-1])
        ct.append(cot_in_ref[:, g * BLK : g * BLK + BLK])
    hi, lo, ct = hi + [zero], lo + [zero], ct + [zero]
    for g in range(n):
        p, c, q = g, g + 1, g + 2
        around = jnp.where(lane < 64, hi[q], hi[p])
        around = jnp.where(jnp.logical_and(lane >= 32, lane < 96), jnp.where(
            lane < 64, pltpu.roll(lo[q], 32, 1), pltpu.roll(lo[p], BLK - 32, 1)), around)
        around = jnp.where(jnp.logical_and(lane >= 40, lane < 88), jnp.where(
            lane < 64, pltpu.roll(ct[q], 40, 1), pltpu.roll(ct[p], BLK - 40, 1)), around)
        send_e[g] = jnp.concatenate([hi[c], around, lo[c], ct[c]], axis=1).astype(BF16)
    pl.semaphore_wait(barrier, n - 1)
    copies_e = exchange(0, lambda to: send_e.at[to], recv_e)
    recv_e[me] = send_e[me]
    for copy in loads[2:]:
        copy.wait()

    psf = psf_ref[...]
    norm = psf / jnp.sum(psf, axis=1, keepdims=True)
    bank = iota((8, TAPS), 0)
    left, right = jnp.maximum(me - 1, 0), jnp.minimum(me + 1, n - 1)

    def taps_of(which, blk, group):
        k = pick_ref[which, zone_ref[blk, group]]
        return jnp.sum(jnp.where(bank == k, norm, 0.0), axis=0, keepdims=True)

    def banded(parts, wide, at):
        ahead = at % 8
        lines = []
        for taps, count in parts:
            line = [taps, jnp.zeros((1, wide - TAPS - ahead), F32)]
            line = jnp.concatenate([jnp.zeros((1, ahead), F32)] * (ahead > 0) + line, axis=1)
            lines.append(jnp.broadcast_to(line, (count, wide)))
        lines = lines[0] if len(lines) == 1 else jnp.concatenate(lines, axis=0)
        return pltpu.roll(lines, (at - ahead) % wide, 1, stride=1, stride_axis=0)

    for blk in range(blocks):
        parts = [
            (jnp.where(first, 0.0, taps_of(0, blk, left)), EDGE), (taps_of(0, blk, me), BLK),
            (jnp.where(last, 0.0, taps_of(0, blk, right)), EDGE)]
        tt[blk] = banded(parts, 256, -28).astype(BF16)
        turned = jnp.concatenate([banded(parts, 256, -24), jnp.zeros((256 - WIDE, 256), F32)], axis=0).T
        t2[blk] = (turned[0:144, 0:WIDE] * -STEP_SIZE).astype(BF16)
        lane = iota((WIDE, 256), 1)
        gone = jnp.logical_or(jnp.logical_and(lane < NEAR, first), jnp.logical_and(lane >= NEAR + BLK, last))
        tg[blk] = jnp.where(gone, 0.0, banded(parts, 256, 4)).astype(BF16)

    def column_operator(group):
        parts = [(taps_of(1, blk, group), BLK) for blk in range(blocks)]
        return banded(parts, height + BLK, -RAD)[:, 0:height]

    own = column_operator(me)
    target = tn_dot(obs_ref[...].astype(BF16), own.astype(BF16))
    strip[0] = target[BLK - EDGE : BLK, :].astype(BF16)
    strip[1] = target[0:EDGE, :].astype(BF16)
    copies_o = neighbours(0, strip, halo)
    slab[0:BLK, :] = target
    for i, op in enumerate((column_operator(left), own, column_operator(right))):
        mats[i] = tn_dot(op, op, precision=lax.Precision.HIGHEST).astype(BF16)
    build_weights(wf_ref, wl_ref, w9_ref, w1, wlt, wl3, wf3, wmb, wmtb)
    row, lane = iota((144, 384), 0), iota((144, 384), 1)
    rest = jnp.where(row < 4, row + 220, jnp.where(row < 132, row + 252, row + 28))
    sel = ones_where(jnp.logical_or(jnp.bitwise_and(row - 4, 255) == lane, rest == lane))
    row, lane = iota((144, 256), 0), iota((144, 256), 1)
    sel_c = ones_where(jnp.where(row < 4, row + 212, jnp.where(row < 132, row - 4, row + 36)) == lane)
    eye = ones_where(iota((BLK, BLK), 0) == iota((BLK, BLK), 1))

    def twice(v):
        return jnp.concatenate(
            [dot(v[0:EDGE], mats[0]), dot(v[EDGE : EDGE + BLK], mats[1]), dot(v[EDGE + BLK : WIDE], mats[2])], axis=0)

    def gather(blk):
        per = BLK // BAND
        return jnp.concatenate([recv_e[blk * per + i].astype(F32) for i in range(per)], axis=0).astype(BF16)

    def joined(parts):
        return parts[0] if len(parts) == 1 else jnp.concatenate(parts, axis=1)

    def halves(v):
        low = jnp.concatenate([v[0:72], v[64:136]], axis=1)
        return jnp.concatenate([low, jnp.zeros((8, lanes), F32)], axis=0)

    arrive(copies_e)
    est = [gather(blk) for blk in range(blocks)]
    blurred = joined([nt_dot(tt[blk], est[blk][:, 0:256]) for blk in range(blocks)]).astype(BF16)
    arrive(copies_o)
    target = jnp.concatenate([halo[0].astype(F32), slab[0:BLK, :], halo[1].astype(F32)], axis=0)
    spread = (twice(blurred) - target).astype(BF16)
    row = iota((144, height), 0)
    outside = jnp.logical_or(jnp.logical_and(row < 4, first), jnp.logical_and(row >= 4 + BLK, last))
    change = joined([dot(t2[blk], spread[:, blk * BLK : blk * BLK + BLK]) for blk in range(blocks)])
    rp_ref[...] = change
    ds = joined([nt_dot(sel, est[blk][:, 0:384]) for blk in range(blocks)]) + change
    ds = halves(jnp.where(outside, 0.0, ds))
    for a in range(3):
        line = ds if a == 1 else moved(ds, a - 1, height)
        for w in range(9):
            fw[w, a * 16 : a * 16 + 16, :] = line[8 * w : 8 * w + 16].astype(BF16)

    cot = joined([
        nt_dot(sel_c, jnp.concatenate([est[blk][:, 3 * BLK :], est[blk][:, BLK : 2 * BLK]], axis=1))
        for blk in range(blocks)])
    cot_ref[...] = cot
    cot = halves(cot)
    lines = [moved(cot, 1, height), cot, moved(cot, -1, height)]
    pad = jnp.zeros((8, lanes), F32)
    for w in range(12):
        at = 6 * w + 1
        cw[w] = jnp.concatenate([line[at : at + 8] for line in lines] + [pad], axis=0).astype(BF16)

    half = iota((1, lanes), 1) >= height

    def masked(v, start, begin, end):
        col = iota(v.shape, 0) // CH + start
        gone = jnp.logical_or(
            jnp.logical_and(jnp.logical_and(col < begin, first), jnp.logical_not(half)),
            jnp.logical_and(jnp.logical_and(col >= end, last), half))
        return jnp.where(gone, 0.0, v)

    def rows(at, count):
        return pl.ds(at if isinstance(at, int) else pl.multiple_of(at, 64), count)

    def conv_first(w, cols, edge):
        size = cols * CH
        act, slope = silu_pair_of_half(dot(w1[0:size, :], fw[w]))
        if edge:
            act = masked(act, 8 * w, 3, COLS_PRE - 3)
        act = act.astype(BF16)
        at = rows(w * 256, size)
        slope1[at, :] = slope
        x3[0, at, :] = moved(act, -1, height)
        x3[1, at, :] = act
        x3[2, at, :] = moved(act, 1, height)

    def run(body, count, tail):
        body(0, tail[0], True)
        if blocks == 1:
            for w in range(1, count - 1):
                body(w, tail[0], False)
        else:
            @pl.loop(1, count - 1)
            def _(w):
                body(w, tail[0], False)
        body(count - 1, tail[1], True)

    run(conv_first, 9, (8, 6))

    def conv_mid(w, cols, edge):
        size, deep = cols * CH, (cols + 2) * CH
        at = rows(w * 192, size)
        total = dot(wmb[0, 0:size, 0:deep], x3[0, rows(w * 192, deep), :])
        for a in (1, 2):
            total = total + dot(wmb[a, 0:size, 0:deep], x3[a, rows(w * 192, deep), :])
        act, slope = silu_pair_of_half(total)
        back = dot(wlt[0:size, :], cw[w]) * slope
        if edge:
            act = masked(act, 6 * w, 2, COLS_MID - 2)
            back = masked(back, 6 * w, 2, COLS_MID - 2)
        mid[at, :] = act.astype(BF16)
        back = back.astype(BF16)
        x3b[0, at, :] = moved(back, 1, height)
        x3b[1, at, :] = back
        x3b[2, at, :] = moved(back, -1, height)

    run(conv_mid, 12, (6, 2))

    def conv_back(w, cols, edge):
        size, deep = cols * CH, (cols + 2) * CH
        total = dot(wmtb[0, 0:size, 0:deep], x3b[0, rows(w * 192, deep), :])
        for a in (1, 2):
            total = total + dot(wmtb[a, 0:size, 0:deep], x3b[a, rows(w * 192, deep), :])
        total = total * slope1[rows(w * 192 + 64, size), :]
        if edge:
            total = masked(total, 6 * w, 1, COLS_BACK - 1)
        bfr[rows(w * 192, size), :] = total.astype(BF16)

    run(conv_back, 11, (6, 6))

    def assembled(sign):
        low, at, high = [jnp.concatenate([d24[w, a * 8 : a * 8 + 8, :] for w in range(8)], axis=0) for a in range(3)]
        total = at + moved(low, -sign, height) + moved(high, sign, height)
        return jnp.concatenate([total[:, 0:height], total[:, height:lanes]], axis=0)

    for w in range(8):
        d24[w] = dot(wf3[...], bfr[w * 256 : w * 256 + 320, :])
    conv_grad = assembled(-1)
    slab[NEAR : NEAR + BLK, :] = conv_grad + cot_ref[4 : 4 + BLK, :]
    strip_g[0] = slab[BLK : BLK + NEAR, :].astype(BF16)
    strip_g[1] = slab[NEAR : 2 * NEAR, :].astype(BF16)
    copies_g = neighbours(1, strip_g, halo_g)

    def beside(parts):
        return jnp.concatenate(parts, axis=1)

    def last_dot():
        lines = []
        for w in range(11):
            line = cw[w]
            if w in (0, 10):
                drop = 2 if w == 0 else 7
                r = iota((32, 1), 0)
                skip = jnp.logical_or(r == drop, jnp.logical_or(r == drop + 8, r == drop + 16))
                line = line * jnp.where(skip, 0.0, 1.0).astype(BF16)
            lines.append(line)
        return nt_dot(beside(lines), beside([mid[w * 192 : w * 192 + 256, :] for w in range(11)]))

    def first_dot():
        gf_acc[...] = jnp.where(iota((48, 256), 1) >= CH, nt_dot(fw[0], bfr[0:256, :]), 0.0) + nt_dot(
            beside([fw[w] for w in range(1, 8)]), beside([bfr[w * 256 : w * 256 + 256, :] for w in range(1, 8)]))
        gf_acc[:, 0:CH] += nt_dot(fw[8], bfr[2048 : 2048 + CH, :])
        return gf_acc[...]

    per = 10 if blocks == 1 else 2
    for g in range(0, 10, per):
        acts = beside([x3[1, w * 192 + 64 : w * 192 + 320, :] for w in range(g, g + per)])
        backs = beside([x3b[:, w * 192 + 64 : w * 192 + 256, :].reshape(576, lanes) for w in range(g, g + per)])
        total = nt_dot(backs, acts).reshape(3, 192, 256)
        gm_acc[...] = total if g == 0 else gm_acc[...] + total
    gm_acc[:, 0:128, 0:192] += nt_dot(
        x3b[:, 62 * CH : 66 * CH, :].reshape(384, lanes), x3[1, 62 * CH : 68 * CH, :]).reshape(3, 128, 192)

    for a in range(3):
        total = gm_acc[a, 0:32, :]
        for r in range(1, 6):
            total = total + pltpu.roll(gm_acc[a, r * 32 : r * 32 + 32, :], 256 - 32 * r, 1)
        share[a * 32 : a * 32 + 32, :] = total[:, 0:BLK] * scale
    core = lax.rem(me, 2)
    pair = me + 1 - 2 * core

    def part(i):
        return pl.ds(pl.multiple_of(i * 48, 16), 48)

    def to_pair(index, src, dst):
        copy = pltpu.make_async_remote_copy(
            src_ref=src, dst_ref=dst, send_sem=hs.at[2, index], recv_sem=hr.at[2, index],
            device_id={"rows": pair}, device_id_type=MESH)
        copy.start()
        started.append(copy)
        return copy

    copy_s = to_pair(0, share.at[part(1 - core)], share_in)

    ends = []
    for acc, deep, ahead in ((first_dot(), 16, 2), (last_dot(), 8, 2)):
        acc = acc[0 : 3 * deep].reshape(3, deep, 256)
        c, col = iota((3, deep, 256), 1), iota((3, deep, 256), 2) // CH
        for b in range(3):
            hit = c == col + 2 + b if deep == 16 else jnp.logical_and(c >= 2, c - 2 + b == col)
            ends.append(jnp.sum(jnp.where(hit, acc, 0.0), axis=1))
    ends = jnp.concatenate(ends + [jnp.zeros((30, 256), F32)], axis=0)
    ends = ends[:, 0:BLK] + ends[:, BLK:]
    ends = ends + pltpu.roll(ends, 64, 1)
    ends = (ends + pltpu.roll(ends, 32, 1)) * scale

    copy_s.wait_recv()
    number = me // 2
    chip[...] = jnp.where(iota((48, BLK), 1) < 96, share[part(core), :] + share_in[...], ends).astype(BF16)
    copies_t = []
    for k in range(1, n // 2):
        copies_t.append(pltpu.make_async_remote_copy(
            src_ref=chip, dst_ref=chips.at[number],
            send_sem=send_sems.at[1, k - 1], recv_sem=recv_sems.at[1, k - 1],
            device_id={"rows": lax.rem(me + 2 * k, n)}, device_id_type=MESH))
    for copy in copies_t:
        copy.start()
    started.extend(copies_t)
    chips[number] = chip[...]

    for w in range(8):
        d24[w] = dot(wl3[...], mid[w * 256 + 32 : w * 256 + 352, :])
    conv_out = (rp_ref[4 : 4 + BLK, :] + assembled(1)).astype(BF16)
    arrive(copies_g)
    grad = jnp.concatenate([halo_g[0], slab[NEAR : NEAR + BLK, :].astype(BF16), halo_g[1]], axis=0)
    blurred = [dot(tg[blk, :, 0:192], grad[:, blk * BLK : blk * BLK + BLK]) for blk in range(blocks)]
    spread = (twice(joined(blurred).astype(BF16)) * -STEP_SIZE).astype(BF16)
    conv_grad = conv_grad.astype(BF16)
    for blk in range(blocks):
        at = slice(blk * BLK, blk * BLK + BLK)
        change = tn_dot(spread[:, at], tt[blk, :, 0:BLK]) + tn_dot(conv_grad[:, at], eye)
        turned = tn_dot(conv_out[:, at], eye)
        for i in range(BLK // BAND):
            lines = slice(i * 8, i * 8 + 8)
            send_g[blk * (BLK // BAND) + i] = jnp.concatenate([turned[lines], change[lines]], axis=0).astype(BF16)
    copies_b = exchange(2, lambda to: send_g.at[to], back_g)
    back_g[me] = send_g[me]

    arrive(copies_t)
    total = chips[0].astype(F32)
    for i in range(1, n // 2):
        total = total + chips[i].astype(F32)
    whole[part(core), :] = total
    copy_w = to_pair(1, whole.at[part(core)], whole.at[part(core)])
    arrive(copies_b)
    for g in range(n):
        at = slice(g * BLK, g * BLK + BLK)
        back = back_g[g].astype(F32)
        den_ref[:, at] = est_ref[:, at] + back[0:8]
        ge_ref[:, at] = cot_in_ref[:, at] + back[8:16]
    copy_w.wait_recv()
    for slot in range(9):
        a, b = slot // 3, slot % 3
        gm_ref[slot] = whole[a * 32 : a * 32 + 32, b * 32 : b * 32 + 32]
        at = 3 * b + a
        gf_ref[slot] = whole[at : at + 1, 96:BLK] + whole[at + 48 : at + 49, 96:BLK]
        gl_ref[slot] = whole[at + 9 : at + 10, 96:BLK] + whole[at + 57 : at + 58, 96:BLK]
    for copy in started:
        copy.wait_send()


def deliver(*refs):
    sems = refs[-1]
    copies = [pltpu.make_async_copy(refs[i], refs[5 + i], sems.at[i]) for i in range(5)]
    for copy in copies:
        copy.start()
    for copy in copies:
        copy.wait()


def on_device(n, estimate, observed, cotangent, zone_map, bank_pick, psf_bank, w_first, w_mid, w_last):
    width = estimate.shape[1]
    height = BAND * n
    lanes = 2 * height
    blocks = height // BLK
    scale = GRAD_FACTOR / math.sqrt(height * width)
    vmem, hbm = pl.BlockSpec(memory_space=pltpu.VMEM), pl.BlockSpec(memory_space=pltpu.HBM)
    flat = pltpu.VMEM((n, 16, BLK), BF16)
    broad = pltpu.VMEM((n, 8, 4 * BLK), BF16)
    ends = jnp.transpose(w_first, (1, 2, 3, 0)), jnp.transpose(w_last, (0, 2, 3, 1))
    middle = jnp.transpose(w_mid, (2, 3, 0, 1)).reshape(9, CH, CH)
    operands = [
        pltpu.with_memory_space_constraint(v, pltpu.HBM)
        for v in (estimate, observed, cotangent, zone_map, bank_pick, psf_bank, *ends, middle)]
    results = pl.pallas_call(
        functools.partial(kernel, n, scale),
        out_shape=(
            pltpu.VMEM((8, width), F32),
            pltpu.VMEM((8, width), F32),
            pltpu.VMEM((9, CH, CH), F32),
            pltpu.VMEM((9, 1, CH), F32),
            pltpu.VMEM((9, 1, CH), F32),
        ),
        in_specs=[hbm] * 9,
        out_specs=[vmem] * 5,
        scratch_shapes=[
            pltpu.VMEM((8, width), F32),
            pltpu.VMEM((height, BLK), F32),
            pltpu.VMEM((8, width), F32),
            pltpu.SMEM(zone_map.shape, jnp.int32),
            pltpu.SMEM(bank_pick.shape, jnp.int32),
            pltpu.VMEM(psf_bank.shape, F32),
            pltpu.VMEM((1, 3, 3, CH), BF16),
            pltpu.VMEM((1, 3, 3, CH), BF16),
            pltpu.VMEM((9, CH, CH), BF16),
            pltpu.SemaphoreType.DMA((9,)),
            broad, broad, flat, flat,
            pltpu.VMEM((96, BLK), F32),
            pltpu.VMEM((48, BLK), F32),
            pltpu.VMEM((48, BLK), BF16),
            pltpu.VMEM((n // 2, 48, BLK), BF16),
            pltpu.VMEM((96, BLK), F32),
            pltpu.VMEM((2, EDGE, height), BF16),
            pltpu.VMEM((2, EDGE, height), BF16),
            pltpu.VMEM((2, NEAR, height), BF16),
            pltpu.VMEM((2, NEAR, height), BF16),
            pltpu.VMEM((blocks, WIDE, 256), BF16),
            pltpu.VMEM((blocks, 144, WIDE), BF16),
            pltpu.VMEM((blocks, WIDE, 256), BF16),
            pltpu.VMEM((3, height, height), BF16),
            pltpu.VMEM((144, height), F32),
            pltpu.VMEM((144, height), F32),
            pltpu.VMEM((144, height), F32),
            pltpu.VMEM((9, 48, lanes), BF16),
            pltpu.VMEM((12, 32, lanes), BF16),
            pltpu.VMEM((NEAR + BLK, height), F32),
            pltpu.VMEM((256, 48), BF16),
            pltpu.VMEM((192, 32), BF16),
            pltpu.VMEM((24, 320), BF16),
            pltpu.VMEM((24, 320), BF16),
            pltpu.VMEM((3, 192, 256), BF16),
            pltpu.VMEM((3, 192, 256), BF16),
            pltpu.VMEM((COLS_PRE * CH, lanes), F32),
            pltpu.VMEM((3, COLS_PRE * CH, lanes), BF16),
            pltpu.VMEM((3, COLS_MID * CH, lanes), BF16),
            pltpu.VMEM((COLS_MID * CH, lanes), BF16),
            pltpu.VMEM((COLS_BACK * CH, lanes), BF16),
            pltpu.VMEM((8, 24, lanes), F32),
            pltpu.VMEM((3, 192, 256), F32),
            pltpu.VMEM((48, 256), F32),
            pltpu.SemaphoreType.DMA((3, n - 1)),
            pltpu.SemaphoreType.DMA((3, n - 1)),
            pltpu.SemaphoreType.DMA((3, 2)),
            pltpu.SemaphoreType.DMA((3, 2)),
        ],
        compiler_params=pltpu.CompilerParams(
            collective_id=0, has_side_effects=True, vmem_limit_bytes=40 << 20 if height <= 256 else 62 << 20),
    )(*operands)
    denoised, grad_estimate, grad_mid, grad_first, grad_last = pl.pallas_call(
        deliver,
        out_shape=tuple(pltpu.HBM(v.shape, v.dtype) for v in results),
        in_specs=[vmem] * 5,
        out_specs=[hbm] * 5,
        scratch_shapes=[pltpu.SemaphoreType.DMA((5,))],
    )(*[pltpu.with_memory_space_constraint(v, pltpu.VMEM) for v in results])
    grad_mid = jnp.transpose(grad_mid.reshape(3, 3, CH, CH), (2, 3, 0, 1))
    grad_first = jnp.transpose(grad_first.reshape(3, 3, 1, CH), (3, 2, 0, 1))
    grad_last = jnp.transpose(grad_last.reshape(3, 3, 1, CH), (2, 3, 0, 1))
    return denoised, grad_estimate, grad_first, grad_mid, grad_last


def solution(mesh):
    placed = (
        P(("parts", "rows"), None),
        P("parts", "rows"),
        P(("parts", "rows"), None),
        P("parts", None),
        P(), P(), P(), P(), P(),
    )
    return jax.shard_map(
        functools.partial(on_device, mesh.shape["rows"]),
        mesh=mesh,
        in_specs=placed,
        out_specs=(
            P(("parts", "rows"), None),
            P(("parts", "rows"), None),
            P("parts", None, None, None),
            P("parts", None, None, None),
            P("parts", None, None, None),
        ),
        check_vma=False,
    )
```

```python
import functools
import math

import jax
import jax.numpy as jnp
from jax import lax
from jax.experimental import pallas as pl
from jax.experimental.pallas import tpu as pltpu
from jax.sharding import PartitionSpec as P

BLK = 128
RAD = 12
TAPS = 2 * RAD + 1
CH = 32
BAND = 8
STEP_SIZE = 2.0
GRAD_FACTOR = 8.0
MESH = pl.DeviceIdType.MESH
F32 = jnp.float32
BF16 = jnp.bfloat16

EDGE = 16
WIDE = BLK + 2 * EDGE
NEAR = 32
COLS_PRE, COLS_MID, COLS_BACK = 70, 68, 66


def tn_dot(a, b, **kw):
    return lax.dot_general(a, b, (((0,), (0,)), ((), ())), preferred_element_type=F32, **kw)


def nt_dot(a, b):
    return lax.dot_general(a, b, (((1,), (1,)), ((), ())), preferred_element_type=F32)


def dot(a, b, **kw):
    return jnp.dot(a, b, preferred_element_type=F32, **kw)


def iota(shape, dim):
    return lax.broadcasted_iota(jnp.int32, shape, dim)


def third(v, size):
    return (v >= size).astype(jnp.int32) + (v >= 2 * size).astype(jnp.int32)


def ones_where(cond):
    return jnp.where(cond, 1.0, 0.0).astype(BF16)


def silu_pair_of_half(h):
    t = jnp.tanh(h)
    q = 0.5 * t
    act = h + h * t
    return act, (0.5 + q) + act * (0.5 - q)


def moved(v, delta, height):
    parts = []
    for at in range(0, v.shape[1], height):
        part = v[:, at : at + height]
        lane = iota((1, height), 1)
        edge = height - 1 if delta == 1 else 0
        keep = jnp.where(lane == edge, 0.0, 1.0).astype(v.dtype)
        parts.append(pltpu.roll(part, height - 1 if delta == 1 else 1, 1) * keep)
    return jnp.concatenate(parts, axis=1)


def build_weights(wf_ref, wl_ref, w9_ref, w1, wlt, wl3, wf3, wmb, wmtb):
    wf, wl = [
        jnp.concatenate([ref[0, a].astype(F32) for a in range(3)], axis=0).astype(BF16) for ref in (wf_ref, wl_ref)]

    def taps(shape, dim):
        k = iota(shape, dim)
        ka = third(k, 3)
        return ka, k - 3 * ka

    ka, kb = taps((9, 48), 0)
    lane = iota((9, 48), 1)
    la = third(lane, 16)
    lc = lane - 16 * la
    for r in range(8):
        pick = ones_where(jnp.logical_and(ka == la, kb == lc - r)) * 0.5
        w1[r * 32 : r * 32 + 32, :] = tn_dot(wf, pick.astype(BF16)).astype(BF16)
    ka, kb = taps((9, 32), 0)
    lane = iota((9, 32), 1)
    la = third(lane, 8)
    lc = lane - 8 * la
    for r in range(6):
        pick = ones_where(jnp.logical_and(jnp.logical_and(ka == la, lane < 24), kb == r + 2 - lc))
        wlt[r * 32 : r * 32 + 32, :] = tn_dot(wl, pick).astype(BF16)
    ka, kb = taps((24, 9), 1)
    out = iota((24, 9), 0)
    oa = third(out, 8)
    orow = out - 8 * oa
    for q in range(10):
        fwd = ones_where(jnp.logical_and(ka == oa, kb == q - orow))
        wl3[:, q * 32 : q * 32 + 32] = dot(fwd, wl).astype(BF16)
        adj = ones_where(jnp.logical_and(ka == oa, kb == orow + 2 - q))
        wf3[:, q * 32 : q * 32 + 32] = dot(adj, wf).astype(BF16)
    eye = ones_where(iota((32, 32), 0) == iota((32, 32), 1))
    wmb[...] = jnp.zeros_like(wmb)
    wmtb[...] = jnp.zeros_like(wmtb)
    for a in range(3):
        line = jnp.concatenate([w9_ref[a * 3 + b] for b in range(3)], axis=1)
        line = (line.astype(F32) * 0.5).astype(BF16)
        turned = [nt_dot(eye, w9_ref[a * 3 + 2 - q]) for q in range(3)]
        turned = jnp.concatenate(turned, axis=1).astype(BF16)
        for r in range(6):
            wmb[a, r * 32 : r * 32 + 32, r * 32 : r * 32 + 96] = line
            wmtb[a, r * 32 : r * 32 + 32, r * 32 : r * 32 + 96] = turned


def kernel(
    n, scale,
    est_hbm, obs_hbm, cot_hbm, zone_hbm, pick_hbm, psf_hbm, wf_hbm, wl_hbm, w9_hbm,
    den_ref, ge_ref, gm_ref, gf_ref, gl_ref,
    est_ref, obs_ref, cot_in_ref, zone_ref, pick_ref, psf_ref, wf_ref, wl_ref, w9_ref, load_sems,
    send_e, recv_e, send_g, back_g,
    share, share_in, chip, chips, whole,
    strip, halo, strip_g, halo_g,
    tt, t2, tg, mats, ds_ref, rp_ref, cot_ref, fw, cw, slab,
    w1, wlt, wl3, wf3, wmb, wmtb, slope1, x3, x3b, mid, bfr, d24, gm_acc, gf_acc,
    send_sems, recv_sems, hs, hr,
):
    me = lax.axis_index("rows")
    height = BAND * n
    blocks = height // BLK
    width = BLK * n
    lanes = 2 * height
    first, last = me == 0, me == n - 1
    started = []

    def peer(k):
        return lax.rem(me + k, n)

    loads = []
    for i, (src, dst) in enumerate((
            (est_hbm, est_ref), (cot_hbm, cot_in_ref), (zone_hbm, zone_ref), (pick_hbm, pick_ref), (psf_hbm, psf_ref),
            (obs_hbm, obs_ref), (wf_hbm, wf_ref), (wl_hbm, wl_ref), (w9_hbm, w9_ref))):
        loads.append(pltpu.make_async_copy(src, dst, load_sems.at[i]))
        loads[-1].start()

    barrier = pltpu.get_barrier_semaphore()
    for k in range(1, n):
        pl.semaphore_signal(barrier, inc=1, device_id={"rows": peer(k)}, device_id_type=MESH)

    def exchange(index, src_at, dst):
        copies = []
        for k in range(1, n):
            to = peer(k)
            copies.append(pltpu.make_async_remote_copy(
                src_ref=src_at(to), dst_ref=dst.at[me],
                send_sem=send_sems.at[index, k - 1], recv_sem=recv_sems.at[index, k - 1],
                device_id={"rows": to}, device_id_type=MESH))
        for copy in copies:
            copy.start()
        started.extend(copies)
        return copies

    def neighbours(index, src, dst):
        copies = []
        for side, k in ((0, 1), (1, n - 1)):
            copies.append(pltpu.make_async_remote_copy(
                src_ref=src.at[side], dst_ref=dst.at[side],
                send_sem=hs.at[index, side], recv_sem=hr.at[index, side],
                device_id={"rows": peer(k)}, device_id_type=MESH))
        for copy in copies:
            copy.start()
        started.extend(copies)
        return copies

    def arrive(copies):
        for copy in copies:
            copy.wait_recv()

    for copy in loads[0:2]:
        copy.wait()
    lane = iota((BAND, BLK), 1)
    zero = jnp.zeros((BAND, BLK), F32)
    hi, lo, ct = [zero], [zero], [zero]
    for g in range(n):
        own = est_ref[:, g * BLK : g * BLK + BLK]
        hi.append(own.astype(BF16).astype(F32))
        lo.append(own - hi[-1])
        ct.append(cot_in_ref[:, g * BLK : g * BLK + BLK])
    hi, lo, ct = hi + [zero], lo + [zero], ct + [zero]
    for g in range(n):
        p, c, q = g, g + 1, g + 2
        around = jnp.where(lane < 64, hi[q], hi[p])
        around = jnp.where(jnp.logical_and(lane >= 32, lane < 96), jnp.where(
            lane < 64, pltpu.roll(lo[q], 32, 1), pltpu.roll(lo[p], BLK - 32, 1)), around)
        around = jnp.where(jnp.logical_and(lane >= 40, lane < 88), jnp.where(
            lane < 64, pltpu.roll(ct[q], 40, 1), pltpu.roll(ct[p], BLK - 40, 1)), around)
        send_e[g] = jnp.concatenate([hi[c], around, lo[c], ct[c]], axis=1).astype(BF16)
    pl.semaphore_wait(barrier, n - 1)
    copies_e = exchange(0, lambda to: send_e.at[to], recv_e)
    recv_e[me] = send_e[me]
    for copy in loads[2:]:
        copy.wait()

    psf = psf_ref[...]
    norm = psf / jnp.sum(psf, axis=1, keepdims=True)
    bank = iota((8, TAPS), 0)
    left, right = jnp.maximum(me - 1, 0), jnp.minimum(me + 1, n - 1)

    def taps_of(which, blk, group):
        k = pick_ref[which, zone_ref[blk, group]]
        return jnp.sum(jnp.where(bank == k, norm, 0.0), axis=0, keepdims=True)

    def banded(parts, wide, at):
        ahead = at % 8
        lines = []
        for taps, count in parts:
            line = [taps, jnp.zeros((1, wide - TAPS - ahead), F32)]
            line = jnp.concatenate([jnp.zeros((1, ahead), F32)] * (ahead > 0) + line, axis=1)
            lines.append(jnp.broadcast_to(line, (count, wide)))
        lines = lines[0] if len(lines) == 1 else jnp.concatenate(lines, axis=0)
        return pltpu.roll(lines, (at - ahead) % wide, 1, stride=1, stride_axis=0)

    def column_operator(group):
        parts = [(taps_of(1, blk, group), BLK) for blk in range(blocks)]
        return banded(parts, height + BLK, -RAD)[:, 0:height]

    own = column_operator(me)
    target = tn_dot(obs_ref[...].astype(BF16), own.astype(BF16))
    strip[0] = target[BLK - EDGE : BLK, :].astype(BF16)
    strip[1] = target[0:EDGE, :].astype(BF16)
    copies_o = neighbours(0, strip, halo)
    slab[0:BLK, :] = target
    for blk in range(blocks):
        parts = [
            (jnp.where(first, 0.0, taps_of(0, blk, left)), EDGE), (taps_of(0, blk, me), BLK),
            (jnp.where(last, 0.0, taps_of(0, blk, right)), EDGE)]
        tt[blk] = banded(parts, 256, -28).astype(BF16)
        turned = jnp.concatenate([banded(parts, 256, -24), jnp.zeros((256 - WIDE, 256), F32)], axis=0).T
        t2[blk] = (turned[0:144, 0:WIDE] * -STEP_SIZE).astype(BF16)
        lane = iota((WIDE, 256), 1)
        gone = jnp.logical_or(jnp.logical_and(lane < NEAR, first), jnp.logical_and(lane >= NEAR + BLK, last))
        tg[blk] = jnp.where(gone, 0.0, banded(parts, 256, 4)).astype(BF16)

    for i, op in enumerate((column_operator(left), own, column_operator(right))):
        mats[i] = tn_dot(op, op, precision=lax.Precision.HIGHEST).astype(BF16)
    build_weights(wf_ref, wl_ref, w9_ref, w1, wlt, wl3, wf3, wmb, wmtb)
    row, lane = iota((144, 384), 0), iota((144, 384), 1)
    rest = jnp.where(row < 4, row + 220, jnp.where(row < 132, row + 252, row + 28))
    sel = ones_where(jnp.logical_or(jnp.bitwise_and(row - 4, 255) == lane, rest == lane))
    row, lane = iota((144, 256), 0), iota((144, 256), 1)
    sel_c = ones_where(jnp.where(row < 4, row + 212, jnp.where(row < 132, row - 4, row + 36)) == lane)
    eye = ones_where(iota((BLK, BLK), 0) == iota((BLK, BLK), 1))

    def twice(v):
        return jnp.concatenate(
            [dot(v[0:EDGE], mats[0]), dot(v[EDGE : EDGE + BLK], mats[1]), dot(v[EDGE + BLK : WIDE], mats[2])], axis=0)

    def gather(blk):
        per = BLK // BAND
        return jnp.concatenate([recv_e[blk * per + i].astype(F32) for i in range(per)], axis=0).astype(BF16)

    def joined(parts):
        return parts[0] if len(parts) == 1 else jnp.concatenate(parts, axis=1)

    def halves(v):
        low = jnp.concatenate([v[0:72], v[64:136]], axis=1)
        return jnp.concatenate([low, jnp.zeros((8, lanes), F32)], axis=0)

    arrive(copies_e)
    est = [gather(blk) for blk in range(blocks)]
    blurred = joined([nt_dot(tt[blk], est[blk][:, 0:256]) for blk in range(blocks)]).astype(BF16)
    arrive(copies_o)
    target = jnp.concatenate([halo[0].astype(F32), slab[0:BLK, :], halo[1].astype(F32)], axis=0)
    spread = (twice(blurred) - target).astype(BF16)
    row = iota((144, height), 0)
    outside = jnp.logical_or(jnp.logical_and(row < 4, first), jnp.logical_and(row >= 4 + BLK, last))
    change = joined([dot(t2[blk], spread[:, blk * BLK : blk * BLK + BLK]) for blk in range(blocks)])
    rp_ref[...] = change
    ds = joined([nt_dot(sel, est[blk][:, 0:384]) for blk in range(blocks)]) + change
    ds = halves(jnp.where(outside, 0.0, ds))
    for a in range(3):
        line = ds if a == 1 else moved(ds, a - 1, height)
        for w in range(9):
            fw[w, a * 16 : a * 16 + 16, :] = line[8 * w : 8 * w + 16].astype(BF16)

    cot = joined([
        nt_dot(sel_c, jnp.concatenate([est[blk][:, 3 * BLK :], est[blk][:, BLK : 2 * BLK]], axis=1))
        for blk in range(blocks)])
    cot_ref[...] = cot
    cot = halves(cot)
    lines = [moved(cot, 1, height), cot, moved(cot, -1, height)]
    pad = jnp.zeros((8, lanes), F32)
    for w in range(12):
        at = 6 * w + 1
        cw[w] = jnp.concatenate([line[at : at + 8] for line in lines] + [pad], axis=0).astype(BF16)

    half = iota((1, lanes), 1) >= height

    def masked(v, start, begin, end):
        col = iota(v.shape, 0) // CH + start
        gone = jnp.logical_or(
            jnp.logical_and(jnp.logical_and(col < begin, first), jnp.logical_not(half)),
            jnp.logical_and(jnp.logical_and(col >= end, last), half))
        return jnp.where(gone, 0.0, v)

    def rows(at, count):
        return pl.ds(at if isinstance(at, int) else pl.multiple_of(at, 64), count)

    def conv_first(w, cols, edge):
        size = cols * CH
        act, slope = silu_pair_of_half(dot(w1[0:size, :], fw[w]))
        if edge:
            act = masked(act, 8 * w, 3, COLS_PRE - 3)
        act = act.astype(BF16)
        at = rows(w * 256, size)
        slope1[at, :] = slope
        x3[0, at, :] = moved(act, -1, height)
        x3[1, at, :] = act
        x3[2, at, :] = moved(act, 1, height)

    def run(body, count, tail):
        body(0, tail[0], True)
        if blocks == 1:
            for w in range(1, count - 1):
                body(w, tail[0], False)
        else:
            @pl.loop(1, count - 1)
            def _(w):
                body(w, tail[0], False)
        body(count - 1, tail[1], True)

    run(conv_first, 9, (8, 6))

    def conv_mid(w, cols, edge):
        size, deep = cols * CH, (cols + 2) * CH
        at = rows(w * 192, size)
        total = dot(wmb[0, 0:size, 0:deep], x3[0, rows(w * 192, deep), :])
        for a in (1, 2):
            total = total + dot(wmb[a, 0:size, 0:deep], x3[a, rows(w * 192, deep), :])
        act, slope = silu_pair_of_half(total)
        back = dot(wlt[0:size, :], cw[w]) * slope
        if edge:
            act = masked(act, 6 * w, 2, COLS_MID - 2)
            back = masked(back, 6 * w, 2, COLS_MID - 2)
        mid[at, :] = act.astype(BF16)
        back = back.astype(BF16)
        x3b[0, at, :] = moved(back, 1, height)
        x3b[1, at, :] = back
        x3b[2, at, :] = moved(back, -1, height)

    run(conv_mid, 12, (6, 2))

    def conv_back(w, cols, edge):
        size, deep = cols * CH, (cols + 2) * CH
        total = dot(wmtb[0, 0:size, 0:deep], x3b[0, rows(w * 192, deep), :])
        for a in (1, 2):
            total = total + dot(wmtb[a, 0:size, 0:deep], x3b[a, rows(w * 192, deep), :])
        total = total * slope1[rows(w * 192 + 64, size), :]
        if edge:
            total = masked(total, 6 * w, 1, COLS_BACK - 1)
        bfr[rows(w * 192, size), :] = total.astype(BF16)

    run(conv_back, 11, (6, 6))

    def assembled(sign):
        low, at, high = [jnp.concatenate([d24[w, a * 8 : a * 8 + 8, :] for w in range(8)], axis=0) for a in range(3)]
        total = at + moved(low, -sign, height) + moved(high, sign, height)
        return jnp.concatenate([total[:, 0:height], total[:, height:lanes]], axis=0)

    for w in range(8):
        d24[w] = dot(wf3[...], bfr[w * 256 : w * 256 + 320, :])
    conv_grad = assembled(-1)
    slab[NEAR : NEAR + BLK, :] = conv_grad + cot_ref[4 : 4 + BLK, :]
    strip_g[0] = slab[BLK : BLK + NEAR, :].astype(BF16)
    strip_g[1] = slab[NEAR : 2 * NEAR, :].astype(BF16)
    copies_g = neighbours(1, strip_g, halo_g)

    def beside(parts):
        return jnp.concatenate(parts, axis=1)

    def last_dot():
        lines = []
        for w in range(11):
            line = cw[w]
            if w in (0, 10):
                drop = 2 if w == 0 else 7
                r = iota((32, 1), 0)
                skip = jnp.logical_or(r == drop, jnp.logical_or(r == drop + 8, r == drop + 16))
                line = line * jnp.where(skip, 0.0, 1.0).astype(BF16)
            lines.append(line)
        return nt_dot(beside(lines), beside([mid[w * 192 : w * 192 + 256, :] for w in range(11)]))

    def first_dot():
        gf_acc[...] = jnp.where(iota((48, 256), 1) >= CH, nt_dot(fw[0], bfr[0:256, :]), 0.0) + nt_dot(
            beside([fw[w] for w in range(1, 8)]), beside([bfr[w * 256 : w * 256 + 256, :] for w in range(1, 8)]))
        gf_acc[:, 0:CH] += nt_dot(fw[8], bfr[2048 : 2048 + CH, :])
        return gf_acc[...]

    per = 10 if blocks == 1 else 2
    for g in range(0, 10, per):
        acts = beside([x3[1, w * 192 + 64 : w * 192 + 320, :] for w in range(g, g + per)])
        backs = beside([x3b[:, w * 192 + 64 : w * 192 + 256, :].reshape(576, lanes) for w in range(g, g + per)])
        total = nt_dot(backs, acts).reshape(3, 192, 256)
        gm_acc[...] = total if g == 0 else gm_acc[...] + total
    gm_acc[:, 0:128, 0:192] += nt_dot(
        x3b[:, 62 * CH : 66 * CH, :].reshape(384, lanes), x3[1, 62 * CH : 68 * CH, :]).reshape(3, 128, 192)

    for a in range(3):
        total = gm_acc[a, 0:32, :]
        for r in range(1, 6):
            total = total + pltpu.roll(gm_acc[a, r * 32 : r * 32 + 32, :], 256 - 32 * r, 1)
        share[a * 32 : a * 32 + 32, :] = total[:, 0:BLK] * scale
    core = lax.rem(me, 2)
    pair = me + 1 - 2 * core

    def part(i):
        return pl.ds(pl.multiple_of(i * 48, 16), 48)

    def to_pair(index, src, dst):
        copy = pltpu.make_async_remote_copy(
            src_ref=src, dst_ref=dst, send_sem=hs.at[2, index], recv_sem=hr.at[2, index],
            device_id={"rows": pair}, device_id_type=MESH)
        copy.start()
        started.append(copy)
        return copy

    copy_s = to_pair(0, share.at[part(1 - core)], share_in)

    ends = []
    for acc, deep, ahead in ((first_dot(), 16, 2), (last_dot(), 8, 2)):
        acc = acc[0 : 3 * deep].reshape(3, deep, 256)
        c, col = iota((3, deep, 256), 1), iota((3, deep, 256), 2) // CH
        for b in range(3):
            hit = c == col + 2 + b if deep == 16 else jnp.logical_and(c >= 2, c - 2 + b == col)
            ends.append(jnp.sum(jnp.where(hit, acc, 0.0), axis=1))
    ends = jnp.concatenate(ends + [jnp.zeros((30, 256), F32)], axis=0)
    ends = ends[:, 0:BLK] + ends[:, BLK:]
    ends = ends + pltpu.roll(ends, 64, 1)
    ends = (ends + pltpu.roll(ends, 32, 1)) * scale

    copy_s.wait_recv()
    number = me // 2
    chip[...] = jnp.where(iota((48, BLK), 1) < 96, share[part(core), :] + share_in[...], ends).astype(BF16)
    copies_t = []
    for k in range(1, n // 2):
        copies_t.append(pltpu.make_async_remote_copy(
            src_ref=chip, dst_ref=chips.at[number],
            send_sem=send_sems.at[1, k - 1], recv_sem=recv_sems.at[1, k - 1],
            device_id={"rows": lax.rem(me + 2 * k, n)}, device_id_type=MESH))
    for copy in copies_t:
        copy.start()
    started.extend(copies_t)
    chips[number] = chip[...]

    for w in range(8):
        d24[w] = dot(wl3[...], mid[w * 256 + 32 : w * 256 + 352, :])
    conv_out = (rp_ref[4 : 4 + BLK, :] + assembled(1)).astype(BF16)
    arrive(copies_g)
    grad = jnp.concatenate([halo_g[0], slab[NEAR : NEAR + BLK, :].astype(BF16), halo_g[1]], axis=0)
    blurred = [dot(tg[blk, :, 0:192], grad[:, blk * BLK : blk * BLK + BLK]) for blk in range(blocks)]
    spread = (twice(joined(blurred).astype(BF16)) * -STEP_SIZE).astype(BF16)
    conv_grad = conv_grad.astype(BF16)
    for blk in range(blocks):
        at = slice(blk * BLK, blk * BLK + BLK)
        change = tn_dot(spread[:, at], tt[blk, :, 0:BLK]) + tn_dot(conv_grad[:, at], eye)
        turned = tn_dot(conv_out[:, at], eye)
        for i in range(BLK // BAND):
            lines = slice(i * 8, i * 8 + 8)
            send_g[blk * (BLK // BAND) + i] = jnp.concatenate([turned[lines], change[lines]], axis=0).astype(BF16)
    copies_b = exchange(2, lambda to: send_g.at[to], back_g)
    back_g[me] = send_g[me]

    arrive(copies_t)
    total = chips[0].astype(F32)
    for i in range(1, n // 2):
        total = total + chips[i].astype(F32)
    whole[part(core), :] = total
    copy_w = to_pair(1, whole.at[part(core)], whole.at[part(core)])
    arrive(copies_b)
    for g in range(n):
        at = slice(g * BLK, g * BLK + BLK)
        back = back_g[g].astype(F32)
        den_ref[:, at] = est_ref[:, at] + back[0:8]
        ge_ref[:, at] = cot_in_ref[:, at] + back[8:16]
    copy_w.wait_recv()
    for slot in range(9):
        a, b = slot // 3, slot % 3
        gm_ref[slot] = whole[a * 32 : a * 32 + 32, b * 32 : b * 32 + 32]
        at = 3 * b + a
        gf_ref[slot] = whole[at : at + 1, 96:BLK] + whole[at + 48 : at + 49, 96:BLK]
        gl_ref[slot] = whole[at + 9 : at + 10, 96:BLK] + whole[at + 57 : at + 58, 96:BLK]
    for copy in started:
        copy.wait_send()


def deliver(*refs):
    sems = refs[-1]
    copies = [pltpu.make_async_copy(refs[i], refs[5 + i], sems.at[i]) for i in range(5)]
    for copy in copies:
        copy.start()
    for copy in copies:
        copy.wait()


def on_device(n, estimate, observed, cotangent, zone_map, bank_pick, psf_bank, w_first, w_mid, w_last):
    width = estimate.shape[1]
    height = BAND * n
    lanes = 2 * height
    blocks = height // BLK
    scale = GRAD_FACTOR / math.sqrt(height * width)
    vmem, hbm = pl.BlockSpec(memory_space=pltpu.VMEM), pl.BlockSpec(memory_space=pltpu.HBM)
    flat = pltpu.VMEM((n, 16, BLK), BF16)
    broad = pltpu.VMEM((n, 8, 4 * BLK), BF16)
    ends = jnp.transpose(w_first, (1, 2, 3, 0)), jnp.transpose(w_last, (0, 2, 3, 1))
    middle = jnp.transpose(w_mid, (2, 3, 0, 1)).reshape(9, CH, CH)
    operands = [
        pltpu.with_memory_space_constraint(v, pltpu.HBM)
        for v in (estimate, observed, cotangent, zone_map, bank_pick, psf_bank, *ends, middle)]
    results = pl.pallas_call(
        functools.partial(kernel, n, scale),
        out_shape=(
            pltpu.VMEM((8, width), F32),
            pltpu.VMEM((8, width), F32),
            pltpu.VMEM((9, CH, CH), F32),
            pltpu.VMEM((9, 1, CH), F32),
            pltpu.VMEM((9, 1, CH), F32),
        ),
        in_specs=[hbm] * 9,
        out_specs=[vmem] * 5,
        scratch_shapes=[
            pltpu.VMEM((8, width), F32),
            pltpu.VMEM((height, BLK), F32),
            pltpu.VMEM((8, width), F32),
            pltpu.SMEM(zone_map.shape, jnp.int32),
            pltpu.SMEM(bank_pick.shape, jnp.int32),
            pltpu.VMEM(psf_bank.shape, F32),
            pltpu.VMEM((1, 3, 3, CH), BF16),
            pltpu.VMEM((1, 3, 3, CH), BF16),
            pltpu.VMEM((9, CH, CH), BF16),
            pltpu.SemaphoreType.DMA((9,)),
            broad, broad, flat, flat,
            pltpu.VMEM((96, BLK), F32),
            pltpu.VMEM((48, BLK), F32),
            pltpu.VMEM((48, BLK), BF16),
            pltpu.VMEM((n // 2, 48, BLK), BF16),
            pltpu.VMEM((96, BLK), F32),
            pltpu.VMEM((2, EDGE, height), BF16),
            pltpu.VMEM((2, EDGE, height), BF16),
            pltpu.VMEM((2, NEAR, height), BF16),
            pltpu.VMEM((2, NEAR, height), BF16),
            pltpu.VMEM((blocks, WIDE, 256), BF16),
            pltpu.VMEM((blocks, 144, WIDE), BF16),
            pltpu.VMEM((blocks, WIDE, 256), BF16),
            pltpu.VMEM((3, height, height), BF16),
            pltpu.VMEM((144, height), F32),
            pltpu.VMEM((144, height), F32),
            pltpu.VMEM((144, height), F32),
            pltpu.VMEM((9, 48, lanes), BF16),
            pltpu.VMEM((12, 32, lanes), BF16),
            pltpu.VMEM((NEAR + BLK, height), F32),
            pltpu.VMEM((256, 48), BF16),
            pltpu.VMEM((192, 32), BF16),
            pltpu.VMEM((24, 320), BF16),
            pltpu.VMEM((24, 320), BF16),
            pltpu.VMEM((3, 192, 256), BF16),
            pltpu.VMEM((3, 192, 256), BF16),
            pltpu.VMEM((COLS_PRE * CH, lanes), F32),
            pltpu.VMEM((3, COLS_PRE * CH, lanes), BF16),
            pltpu.VMEM((3, COLS_MID * CH, lanes), BF16),
            pltpu.VMEM((COLS_MID * CH, lanes), BF16),
            pltpu.VMEM((COLS_BACK * CH, lanes), BF16),
            pltpu.VMEM((8, 24, lanes), F32),
            pltpu.VMEM((3, 192, 256), F32),
            pltpu.VMEM((48, 256), F32),
            pltpu.SemaphoreType.DMA((3, n - 1)),
            pltpu.SemaphoreType.DMA((3, n - 1)),
            pltpu.SemaphoreType.DMA((3, 2)),
            pltpu.SemaphoreType.DMA((3, 2)),
        ],
        compiler_params=pltpu.CompilerParams(
            collective_id=0, has_side_effects=True, vmem_limit_bytes=40 << 20 if height <= 256 else 62 << 20),
    )(*operands)
    denoised, grad_estimate, grad_mid, grad_first, grad_last = pl.pallas_call(
        deliver,
        out_shape=tuple(pltpu.HBM(v.shape, v.dtype) for v in results),
        in_specs=[vmem] * 5,
        out_specs=[hbm] * 5,
        scratch_shapes=[pltpu.SemaphoreType.DMA((5,))],
    )(*[pltpu.with_memory_space_constraint(v, pltpu.VMEM) for v in results])
    grad_mid = jnp.transpose(grad_mid.reshape(3, 3, CH, CH), (2, 3, 0, 1))
    grad_first = jnp.transpose(grad_first.reshape(3, 3, 1, CH), (3, 2, 0, 1))
    grad_last = jnp.transpose(grad_last.reshape(3, 3, 1, CH), (2, 3, 0, 1))
    return denoised, grad_estimate, grad_first, grad_mid, grad_last


def solution(mesh):
    placed = (
        P(("parts", "rows"), None),
        P("parts", "rows"),
        P(("parts", "rows"), None),
        P("parts", None),
        P(), P(), P(), P(), P(),
    )
    return jax.shard_map(
        functools.partial(on_device, mesh.shape["rows"]),
        mesh=mesh,
        in_specs=placed,
        out_specs=(
            P(("parts", "rows"), None),
            P(("parts", "rows"), None),
            P("parts", None, None, None),
            P("parts", None, None, None),
            P("parts", None, None, None),
        ),
        check_vma=False,
    )
```
